128 devices in a mesh: seq: 32 (over y_lo, z, x), head: 4 (over y_hi, core).
Axes of the slice: x: 4, y: 4 (y_hi: 2, y_lo: 2; y = y_hi * 2 + y_lo), z: 4, core: 2. Of those that a mesh axis runs over, the one named last changes fastest.
Arguments:
- tokens: bfloat16 [4096, 7168], P('seq', 'head'), may hold values from -6 to 6
- latent_down: bfloat16 [7168, 576], P('head'), may hold values from -0.0625 to 0.0625
- latent_gain: float32 [512], replicated, may hold values from 0.5 to 1.5
- query_nope: bfloat16 [4096, 8192], P('seq', 'head'), may hold values from -200 to 200
- query_rope: bfloat16 [4096, 4096], P('seq', 'head'), may hold values from -6 to 6
- key_up: bfloat16 [64, 128, 512], P('head'), may hold values from -0.5 to 0.5
- value_up: bfloat16 [64, 512, 128], P('head'), may hold values from -0.25 to 0.25
- prefix_latent: bfloat16 [2048, 576], P('seq'), may hold values from -6 to 6
- prefix_length: int32 [1], replicated, may hold values from 1024 to 2048
- page_table: int32 [256], replicated, may hold values from 0 to 255, each once
Outputs:
- attended: bfloat16 [4096, 8192], P('seq', 'head')
- decode_pool: bfloat16 [256, 9216], P('seq')
The draws below stay inside these ranges and needn't reach their ends.
Inputs may be any that keep to these rules, and one draw needn't show every extreme that they name: The prefix rows from prefix_length[0] on are not live. `page_table`: A permutation of the 256 decode slots.
All inputs are finite; a program needn't handle non-finite values.
Results may differ from the reference program's by a relative error of at most 0.015.
Values may be sent and summed in bfloat16 or wider, within the bound.
A program may use at most 128 MiB of HBM per device.

```python
import jax
import jax.numpy as jnp
from jax import lax

D = 7168
LATENT = 512
ROPE = 64
NOPE = 128
VHEAD = 128
HEADS = 64
PAGE = 16
TOK_DEV = 128
TOKENS = 4096
PREFIX = 2048
PAGES = 256
N_SEQ = 32


def draw_query_nope(key, part):
    first_key = jax.random.fold_in(jax.random.fold_in(key, 17), 0)
    values = jax.random.normal(first_key, (TOKENS, HEADS, NOPE), jnp.float32)
    values = jnp.clip(values, -6.0, 6.0)
    return values.reshape(TOKENS, HEADS * NOPE).astype(jnp.bfloat16)


def steps_of(stream_key, dims, shards, smallest, largest):
    gain, own = 1.0, jax.random.fold_in(stream_key, 6)
    for position, blocks in shards:
        draws = jnp.exp(jax.random.uniform(jax.random.fold_in(own, position), (blocks,), jnp.float32, smallest / len(shards), largest / len(shards)))
        gain = gain * jnp.repeat(draws, dims[position] // blocks).reshape([-1 if axis == position else 1 for axis in range(len(dims))])
    return gain


def gaussian(own_key, extent, scale, limit, cuts=(), kind=jnp.bfloat16):
    entries = scale * jax.random.normal(own_key, extent, jnp.float32)
    if cuts:
        entries = entries * steps_of(own_key, extent, cuts, -0.22, 0.18)
    return jnp.clip(entries, -limit, limit).astype(kind)


def setup_inputs(seed: int = 0) -> dict:
    seeds = jax.random.split(jax.random.key(seed), 11)
    tokens = gaussian(seeds[0], (TOKENS, D), 1.0, 6.0, ((0, 32), (1, 4)))
    latent_down = gaussian(seeds[1], (D, LATENT + ROPE), D ** -0.5, 0.0625, ((0, 4),))
    latent_gain = jnp.clip(1.0 + 0.1 * jax.random.normal(seeds[2], (LATENT,), jnp.float32), 0.5, 1.5)
    query_nope = draw_query_nope(jax.random.fold_in(seeds[10], 71), 0)
    query_rope = gaussian(seeds[4], (TOKENS, HEADS * ROPE), 1.0, 6.0, ((0, 32), (1, 4)))
    key_up = gaussian(seeds[5], (HEADS, NOPE, LATENT), NOPE ** -0.5, 0.5, ((0, 4),))
    value_up = gaussian(seeds[6], (HEADS, LATENT, VHEAD), LATENT ** -0.5, 0.25, ((0, 4),))
    prefix_latent = gaussian(seeds[7], (PREFIX, LATENT + ROPE), 1.0, 6.0, ((0, 32),))
    prefix_length = jax.random.randint(seeds[8], (1,), PREFIX // 2, PREFIX + 1).astype(jnp.int32)
    page_table = jax.random.permutation(seeds[9], PAGES).astype(jnp.int32)
    return {"tokens": tokens, "latent_down": latent_down, "latent_gain": latent_gain, "query_nope": query_nope, "query_rope": query_rope, "key_up": key_up, "value_up": value_up, "prefix_latent": prefix_latent, "prefix_length": prefix_length, "page_table": page_table}


def angles(positions):
    half_width = ROPE // 2
    frequency = 10000.0 ** (-jnp.arange(half_width, dtype=jnp.float32) / half_width)
    return positions.astype(jnp.float32)[:, None] * frequency[None, :]

def rotate(values, angle_table):
    half_width = values.shape[-1] // 2
    first = values[..., :half_width]
    second = values[..., half_width:]
    cosine = jnp.cos(angle_table)
    sinus = jnp.sin(angle_table)
    return jnp.concatenate([first * cosine - second * sinus, first * sinus + second * cosine], axis=-1)

def finish(mixed, latent_gain, positions):
    latent = mixed[:, :LATENT]
    rope_part = mixed[:, LATENT:]
    normed = latent * lax.rsqrt(lax.optimization_barrier(jnp.mean(latent * latent, axis=1, keepdims=True)) + 1e-06) * latent_gain
    return jnp.concatenate([normed.astype(jnp.bfloat16), rotate(rope_part, angles(positions)).astype(jnp.bfloat16)], axis=1)

def reference(tokens, latent_down, latent_gain, query_nope, query_rope, key_up, value_up, prefix_latent, prefix_length, page_table):
    offset = prefix_length[0]
    positions = offset + jnp.arange(TOKENS, dtype=jnp.int32)
    mixed = jnp.dot(tokens, latent_down, preferred_element_type=jnp.float32)
    new_keys = finish(mixed, latent_gain, positions)
    all_keys = jnp.concatenate([prefix_latent, new_keys], axis=0).astype(jnp.float32)
    value_rows = all_keys[:, :LATENT]
    lifted = jnp.einsum('thn,hnl->thl', query_nope.reshape(TOKENS, HEADS, NOPE).astype(jnp.float32), key_up.astype(jnp.float32)).astype(jnp.bfloat16)
    turned = rotate(query_rope.reshape(TOKENS, HEADS, ROPE).astype(jnp.float32), angles(positions)[:, None, :]).astype(jnp.bfloat16)
    queries = jnp.concatenate([lifted, turned], axis=2)
    key_index = jnp.arange(PREFIX + TOKENS, dtype=jnp.int32)
    score_scale = (NOPE + ROPE) ** (-0.5)

    def one_block(block_index):
        rows = lax.dynamic_slice_in_dim(queries, block_index * TOK_DEV, TOK_DEV, 0).reshape(TOK_DEV * HEADS, LATENT + ROPE).astype(jnp.float32)
        scores = jnp.dot(all_keys, rows.T, precision=lax.Precision.HIGHEST) * score_scale
        query_token = block_index * TOK_DEV + jnp.arange(TOK_DEV * HEADS, dtype=jnp.int32) // HEADS
        in_prefix = key_index[:, None] < PREFIX
        live_mask = jnp.where(in_prefix, key_index[:, None] < offset, key_index[:, None] - PREFIX <= query_token[None, :])
        best = lax.optimization_barrier(jnp.max(jnp.where(live_mask, scores, -jnp.inf), axis=0))
        weights = jnp.where(live_mask, jnp.exp(scores - best[None, :]), 0.0)
        denominator = lax.optimization_barrier(jnp.sum(weights, axis=0))
        rounded = weights.astype(jnp.bfloat16).astype(jnp.float32)
        summed = lax.dot_general(rounded, value_rows, (((0,), (0,)), ((), ())), precision=lax.Precision.HIGHEST)
        attention = (summed / denominator[:, None]).astype(jnp.bfloat16).reshape(TOK_DEV, HEADS, LATENT)
        output = jnp.einsum('thl,hlv->thv', attention.astype(jnp.float32), value_up.astype(jnp.float32))
        return output.reshape(TOK_DEV, HEADS * VHEAD).astype(jnp.bfloat16)
    attended = lax.map(one_block, jnp.arange(N_SEQ, dtype=jnp.int32)).reshape(TOKENS, HEADS * VHEAD)
    pages = new_keys.reshape(PAGES, PAGE * (LATENT + ROPE))
    decode_pool = jnp.zeros_like(pages).at[page_table].set(pages)
    return (attended, decode_pool)
```

```python
import functools
import jax
import jax.numpy as jnp
from jax import lax
from jax.experimental import pallas as pl
from jax.experimental.pallas import tpu as pltpu
from jax.sharding import PartitionSpec as P
LATENT, ROPE, NOPE, VHEAD, PAGE = 512, 64, 128, 128, 16
WIDTH = LATENT + ROPE
ORDERS = (("x", "y", "z"), ("y", "z", "x"), ("z", "x", "y"))
LANES = (pl.ds(0, 256), pl.ds(256, 256), pl.ds(512, 64))
ALL = slice(None)


def place(chip, core):
    y_hi, y_lo = chip["y"] // 2, chip["y"] % 2
    return {"seq": y_lo * 16 + chip["z"] * 4 + chip["x"], "head": y_hi * 2 + core}


def view(buf, chip, core, lanes):
    y = chip["y"]
    y_lo, y_hi = (ALL, ALL) if isinstance(y, slice) else (y % 2, y // 2)
    return buf.at[y_lo, chip["z"], chip["x"], y_hi, core, :, lanes]


class Spread:
    def __init__(self, buf, lanes, order, here, core, send, recv):
        self.buf, self.lanes, self.order = buf, lanes, order
        self.here, self.core, self.send, self.recv = here, core, send, recv

    def copy(self, chip, slot, to, core):
        ref = view(self.buf, chip, self.core, self.lanes)
        return pltpu.make_async_remote_copy(
            src_ref=ref, dst_ref=ref, send_sem=self.send.at[slot], recv_sem=self.recv.at[slot],
            device_id=place(to, core), device_id_type=pl.DeviceIdType.MESH)

    def landed(self, chip, slot):
        ref = view(self.buf, chip, self.core, self.lanes)
        pltpu.make_async_remote_copy(
            src_ref=ref, dst_ref=ref, send_sem=self.send.at[slot], recv_sem=self.recv.at[slot],
            device_id=place(self.here, 1 - self.core), device_id_type=pl.DeviceIdType.MESH).wait_recv()

    def shifted(self, dim, j):
        return {**self.here, dim: (self.here[dim] + j + 4) % 4}

    def group(self, depth, chip):
        return {**chip, **{d: ALL for d in self.order[:depth]}}

    def half(self, chip, k):
        dim = [d for d in self.order[:2] if d != "y"][0]
        return {**self.group(2, chip), dim: pl.ds(2 * k, 2)}

    def ring(self, depth):
        dim = self.order[depth]
        for j in (1, 3, 2):
            self.copy(self.group(depth, self.here), 3 * depth + j - 1, self.shifted(dim, j), self.core).start()

    def ring_landed(self, depth):
        dim = self.order[depth]
        for j in (1, 3, 2):
            self.landed(self.group(depth, self.shifted(dim, -j)), 3 * depth + j - 1)

    def last(self):
        dim = self.order[2]
        right, left = self.shifted(dim, 1), self.shifted(dim, -1)
        self.copy(self.half(self.here, 0), 6, right, self.core).start()
        self.copy(self.half(self.here, 1), 7, left, self.core).start()
        self.copy(self.half(self.here, 1), 8, right, self.core).start()
        self.copy(self.half(self.here, 0), 9, left, self.core).start()
        self.other(self.here, 12)

    def other(self, chip, slot):
        self.copy(self.group(2, chip), slot, self.here, 1 - self.core).start()

    def forward(self):
        dim = self.order[2]
        right, left = self.shifted(dim, 1), self.shifted(dim, -1)
        self.landed(self.half(left, 0), 6)
        self.copy(self.half(left, 0), 10, right, self.core).start()
        self.landed(self.half(right, 1), 7)
        self.copy(self.half(right, 1), 11, left, self.core).start()

    def sides(self):
        dim = self.order[2]
        right, left = self.shifted(dim, 1), self.shifted(dim, -1)
        self.landed(self.half(left, 1), 8)
        self.other(left, 13)
        self.landed(self.half(right, 0), 9)
        self.other(right, 14)

    def far(self):
        far = self.shifted(self.order[2], 2)
        self.landed(self.half(far, 0), 10)
        self.landed(self.half(far, 1), 11)
        self.other(far, 15)

    def others_landed(self):
        dim = self.order[2]
        for j, slot in ((0, 12), (-1, 13), (1, 14), (2, 15)):
            chip = self.group(2, self.shifted(dim, j))
            ref = view(self.buf, chip, 1 - self.core, self.lanes)
            pltpu.make_async_remote_copy(
                src_ref=ref, dst_ref=ref, send_sem=self.send.at[slot], recv_sem=self.recv.at[slot],
                device_id=place(self.here, 1 - self.core), device_id_type=pl.DeviceIdType.MESH).wait_recv()

    def sent(self):
        dim = self.order[2]
        right, left, far = self.shifted(dim, 1), self.shifted(dim, -1), self.shifted(dim, 2)
        for depth in (0, 1):
            for j in (1, 2, 3):
                self.copy(self.group(depth, self.here), 3 * depth + j - 1, self.shifted(self.order[depth], j), self.core).wait_send()
        for slot, chip, k, to in ((6, self.here, 0, right), (7, self.here, 1, left), (8, self.here, 1, right), (9, self.here, 0, left), (10, left, 0, right), (11, right, 1, left)):
            self.copy(self.half(chip, k), slot, to, self.core).wait_send()
        for slot, chip in ((12, self.here), (13, left), (14, right), (15, far)):
            self.copy(self.group(2, chip), slot, self.here, 1 - self.core).wait_send()


def position():
    seq, head = lax.axis_index("seq"), lax.axis_index("head")
    here = {"x": seq % 4, "y": (head // 2) * 2 + seq // 16, "z": (seq // 4) % 4}
    return here, head % 2, head


def greet(here, core):
    barrier = pltpu.get_barrier_semaphore()
    peers = [({**here, d: (here[d] + j) % 4}, core) for d in "xyz" for j in (1, 2, 3)]
    peers += [(here, 1 - core), ({**here, "y": (here["y"] + 2) % 4}, 1 - core)]
    for chip, c in peers:
        pl.semaphore_signal(barrier, inc=1, device_id=place(chip, c), device_id_type=pl.DeviceIdType.MESH)
    pl.semaphore_wait(barrier, len(peers))


def finish(mixed, gain, cos, sin):
    latent, a, b = mixed[:, :LATENT], mixed[:, LATENT : LATENT + 32], mixed[:, LATENT + 32 :]
    normed = latent * lax.rsqrt(jnp.mean(latent * latent, axis=1, keepdims=True) + 1e-06) * gain
    return jnp.concatenate([normed, a * cos - b * sin, a * sin + b * cos], axis=1).astype(jnp.bfloat16)


def gather_kernel(tok_ref, down_ref, gain_ref, cos_ref, sin_ref, pre_ref, pre_out, new_out,
                  pbuf, nbuf, part, parts, own_sem, send, recv, rs_send, rs_recv, out_sem):
    here, core, head = position()
    rows = nbuf.shape[5]
    prow = pbuf.shape[5]
    mine = (here["y"] % 2, here["z"], here["x"], here["y"] // 2, core)
    own = pltpu.make_async_copy(pre_ref.at[pl.ds(head * prow, prow), :], pbuf.at[mine], own_sem)
    own.start()
    greet(here, core)
    own.wait()
    pre = [Spread(pbuf, LANES[i], ORDERS[i], here, core, send.at[i], recv.at[i]) for i in range(3)]
    new = [Spread(nbuf, LANES[i], ORDERS[(i + 1) % 3], here, core, send.at[3 + i], recv.at[3 + i]) for i in range(3)]
    def each(group, name, *args):
        for item in group:
            getattr(item, name)(*args)
    each(pre, "ring", 0)
    term = jnp.dot(tok_ref[...], down_ref[...], preferred_element_type=jnp.float32)
    part[...] = term.astype(jnp.bfloat16)
    def share(j):
        to = (head + j) % 4
        return pltpu.make_async_remote_copy(
            src_ref=part.at[pl.ds(to * rows, rows), :], dst_ref=parts.at[j - 1], send_sem=rs_send.at[j - 1], recv_sem=rs_recv.at[j - 1],
            device_id={"seq": lax.axis_index("seq"), "head": to}, device_id_type=pl.DeviceIdType.MESH)
    for j in (1, 2, 3):
        share(j).start()
    each(pre, "ring_landed", 0)
    each(pre, "ring", 1)
    for j in (1, 2, 3):
        share(j).wait_recv()
    mixed = part[pl.ds(pl.multiple_of(head * rows, rows), rows), :].astype(jnp.float32)
    for j in range(3):
        mixed += parts[j].astype(jnp.float32)
    nbuf[mine] = finish(mixed, gain_ref[...], cos_ref[...], sin_ref[...])
    each(new, "ring", 0)
    each(pre, "ring_landed", 1)
    each(pre, "last")
    each(new, "ring_landed", 0)
    each(new, "ring", 1)
    each(pre, "forward")
    each(new, "ring_landed", 1)
    each(new, "last")
    each(pre, "sides")
    each(pre, "far")
    each(new, "forward")
    each(new, "sides")
    each(pre, "others_landed")
    out_p = pltpu.make_async_copy(pbuf, pre_out, out_sem.at[0])
    out_p.start()
    each(new, "far")
    each(new, "others_landed")
    out_n = pltpu.make_async_copy(nbuf, new_out, out_sem.at[1])
    out_n.start()
    each(pre, "sent")
    each(new, "sent")
    for j in (1, 2, 3):
        share(j).wait_send()
    out_p.wait()
    out_n.wait()


def gather(tokens, down, gain, cos, sin, prefix):
    rows, prow = tokens.shape[0] // 4, prefix.shape[0] // 4
    vm, hbm = pl.BlockSpec(memory_space=pltpu.VMEM), pl.BlockSpec(memory_space=pl.ANY)
    grid = (2, 4, 4, 2, 2)
    return pl.pallas_call(gather_kernel,
        out_shape=[jax.ShapeDtypeStruct((*grid, prow, WIDTH), jnp.bfloat16), jax.ShapeDtypeStruct((*grid, rows, WIDTH), jnp.bfloat16)],
        in_specs=[vm] * 5 + [hbm], out_specs=[hbm, hbm],
        scratch_shapes=[pltpu.VMEM((*grid, prow, WIDTH), jnp.bfloat16), pltpu.VMEM((*grid, rows, WIDTH), jnp.bfloat16),
            pltpu.VMEM((4 * rows, WIDTH), jnp.bfloat16), pltpu.VMEM((3, rows, WIDTH), jnp.bfloat16), pltpu.SemaphoreType.DMA,
            pltpu.SemaphoreType.DMA((6, 16)), pltpu.SemaphoreType.DMA((6, 16)), pltpu.SemaphoreType.DMA((3,)), pltpu.SemaphoreType.DMA((3,)), pltpu.SemaphoreType.DMA((2,))],
        compiler_params=pltpu.CompilerParams(vmem_limit_bytes=60 << 20, collective_id=0, has_side_effects=True), name="gather")(tokens, down, gain, cos, sin, prefix)


KB = 512
SCALE = (NOPE + ROPE) ** -0.5 * 1.4426950408889634
NEG = -1e30

def attn_kernel(heads, toks, n_pre, sc_ref, qn_ref, qr_ref, cos_ref, sin_ref, ku_ref, vu_ref, k_ref, out_ref, qt, acc, m_s, l_s, sb, vt):
    nq = heads * toks
    plen = sc_ref[0]
    first_row = sc_ref[1]
    pre_blocks = (plen + KB - 1) // KB
    own_blocks = (first_row + toks + KB - 1) // KB
    total = pre_blocks + own_blocks
    cos, sin = cos_ref[...], sin_ref[...]
    for h in range(heads):
        cols = pl.ds(h * toks, toks)
        lifted = jnp.dot(qn_ref[:, pl.ds(h * NOPE, NOPE)], ku_ref[h], preferred_element_type=jnp.float32)
        qt[:LATENT, cols] = lifted.T.astype(jnp.bfloat16)
    for g in range(heads // 2):
        both = qr_ref[:, pl.ds(g * 128, 128)].astype(jnp.float32).T
        for e in range(2):
            h = 2 * g + e
            a, b = both[64 * e : 64 * e + 32], both[64 * e + 32 : 64 * e + 64]
            cols = pl.ds(h * toks, toks)
            qt[LATENT : LATENT + 32, cols] = (a * cos - b * sin).astype(jnp.bfloat16)
            qt[LATENT + 32 :, cols] = (a * sin + b * cos).astype(jnp.bfloat16)
    m_s[...] = jnp.full_like(m_s, NEG)
    l_s[...] = jnp.zeros_like(l_s)
    acc[...] = jnp.zeros_like(acc)

    def row_of(i):
        return pl.multiple_of(jnp.where(i < pre_blocks, i * KB, n_pre + (i - pre_blocks) * KB), KB)

    def score(i, slot):
        keys = k_ref[pl.ds(row_of(i), KB), :]
        sb[slot] = jnp.dot(keys, qt[...], preferred_element_type=jnp.float32)
        in_pre = i < pre_blocks
        partial = jnp.logical_or(i == total - 1, i == pre_blocks - 1)
        @pl.when(partial)
        def _():
            for h in range(heads):
                cols = pl.ds(h * toks, toks)
                key = lax.broadcasted_iota(jnp.int32, (KB, toks), 0)
                tok = lax.broadcasted_iota(jnp.int32, (KB, toks), 1)
                limit = jnp.where(in_pre, plen - i * KB - 1, first_row - (i - pre_blocks) * KB)
                step = jnp.where(in_pre, 0, 1)
                sb[slot, :, cols] = jnp.where(key <= tok * step + limit, sb[slot, :, cols], NEG)

    def soft(i, slot):
        vt[...] = k_ref[pl.ds(row_of(i), KB), pl.ds(0, LATENT)].T
        s = sb[slot]
        old = m_s[0:1]
        new = jnp.maximum(old, jnp.max(s, axis=0, keepdims=True))
        fade = jnp.exp2((old - new) * SCALE)
        m_s[0:1] = new
        w = jnp.exp2((s - new) * SCALE)
        l_s[0:1] = l_s[0:1] * fade + jnp.sum(w, axis=0, keepdims=True)
        acc[...] = acc[...] * fade + jnp.dot(vt[...], w.astype(jnp.bfloat16), preferred_element_type=jnp.float32)

    score(0, 0)
    def step(pair, carry):
        for u in range(2):
            i = pair * 2 + u
            @pl.when(i < total)
            def _():
                score(jnp.minimum(i + 1, total - 1), 1 - u)
                soft(i, u)
        return carry
    lax.fori_loop(0, (total + 1) // 2, step, 0)
    for h in range(heads):
        cols = pl.ds(h * toks, toks)
        att = (acc[:, cols] / l_s[0:1, cols]).astype(jnp.bfloat16)
        out_ref[:, pl.ds(h * VHEAD, VHEAD)] = lax.dot_general(att, vu_ref[h], (((0,), (0,)), ((), ())), preferred_element_type=jnp.float32).astype(jnp.bfloat16)

def attend(scalars, qn, qr, cos, sin, ku, vu, keys, n_pre):
    heads, toks = ku.shape[0], qn.shape[0]
    nq = heads * toks
    vm = pl.BlockSpec(memory_space=pltpu.VMEM)
    return pl.pallas_call(functools.partial(attn_kernel, heads, toks, n_pre),
        out_shape=jax.ShapeDtypeStruct((toks, heads * VHEAD), jnp.bfloat16),
        in_specs=[pl.BlockSpec(memory_space=pltpu.SMEM)] + [vm] * 7, out_specs=vm,
        scratch_shapes=[pltpu.VMEM((LATENT + ROPE, nq), jnp.bfloat16), pltpu.VMEM((LATENT, nq), jnp.float32), pltpu.VMEM((8, nq), jnp.float32), pltpu.VMEM((8, nq), jnp.float32),
            pltpu.VMEM((2, KB, nq), jnp.float32), pltpu.VMEM((LATENT, KB), jnp.bfloat16)],
        compiler_params=pltpu.CompilerParams(vmem_limit_bytes=60 << 20), name="attend")(scalars, qn, qr, cos, sin, ku, vu, keys)


def tables(positions):
    frequency = 10000.0 ** (-jnp.arange(ROPE // 2, dtype=jnp.float32) / (ROPE // 2))
    angle = positions.astype(jnp.float32)[:, None] * frequency[None, :]
    return jnp.cos(angle), jnp.sin(angle)


def per_device(tokens, latent_down, latent_gain, query_nope, query_rope, key_up, value_up, prefix_latent, prefix_length, page_table):
    toks = tokens.shape[0]
    seq, head = lax.axis_index("seq"), lax.axis_index("head")
    offset = prefix_length[0]
    first_row = seq * toks
    cos, sin = tables(offset + first_row + jnp.arange(toks, dtype=jnp.int32))
    rows = toks // 4
    own_cos = lax.dynamic_slice_in_dim(cos, head * rows, rows)
    own_sin = lax.dynamic_slice_in_dim(sin, head * rows, rows)
    pre, new = gather(tokens, latent_down, latent_gain.reshape(1, LATENT), own_cos, own_sin, prefix_latent)
    keys = jnp.concatenate([pre.reshape(-1, WIDTH), new.reshape(-1, WIDTH)], axis=0)
    scalars = jnp.stack([offset, first_row])
    attended = attend(scalars, query_nope, query_rope, cos.T, sin.T, key_up, value_up, keys, 32 * prefix_latent.shape[0])
    pages = toks // PAGE
    slots = seq * pages + jnp.arange(pages, dtype=jnp.int32)
    wanted = jnp.sum(jnp.where(page_table[None, :] == slots[:, None], jnp.arange(page_table.shape[0], dtype=jnp.int32)[None, :], 0), axis=1)
    pool = new.reshape(page_table.shape[0], PAGE, WIDTH)[wanted].reshape(pages, PAGE * WIDTH)
    return attended, pool


def solution(mesh):
    placed = (P("seq", "head"), P("head", None), P(), P("seq", "head"), P("seq", "head"), P("head", None, None), P("head", None, None), P("seq", None), P(), P())
    return jax.shard_map(per_device, mesh=mesh, in_specs=placed, out_specs=(P("seq", "head"), P("seq", None)), check_vma=False)
```

```python
import functools
import jax
import jax.numpy as jnp
from jax import lax
from jax.experimental import pallas as pl
from jax.experimental.pallas import tpu as pltpu
from jax.sharding import PartitionSpec as P
LATENT, ROPE, NOPE, VHEAD, PAGE = 512, 64, 128, 128, 16
WIDTH = LATENT + ROPE
HALF = ROPE // 2
KB = 512
SCALE = (NOPE + ROPE) ** -0.5 * 1.4426950408889634
NEG = -1e30
ORDERS = (("x", "y", "z"), ("y", "z", "x"), ("z", "x", "y"))
LANES = (pl.ds(0, 256), pl.ds(256, 256), pl.ds(512, 64))
ALL = slice(None)


def place(chip, core):
    y_hi, y_lo = chip["y"] // 2, chip["y"] % 2
    return {"seq": y_lo * 16 + chip["z"] * 4 + chip["x"], "head": y_hi * 2 + core}


def view(buf, chip, core, lanes):
    y = chip["y"]
    y_lo, y_hi = (ALL, ALL) if isinstance(y, slice) else (y % 2, y // 2)
    return buf.at[y_lo, chip["z"], chip["x"], y_hi, core, :, lanes]


class Spread:
    def __init__(self, buf, lanes, order, here, core, send, recv):
        self.buf, self.lanes, self.order = buf, lanes, order
        self.here, self.core, self.send, self.recv = here, core, send, recv

    def copy(self, chip, slot, to, core):
        ref = view(self.buf, chip, self.core, self.lanes)
        return pltpu.make_async_remote_copy(
            src_ref=ref, dst_ref=ref, send_sem=self.send.at[slot], recv_sem=self.recv.at[slot],
            device_id=place(to, core), device_id_type=pl.DeviceIdType.MESH)

    def landed(self, chip, slot):
        ref = view(self.buf, chip, self.core, self.lanes)
        pltpu.make_async_remote_copy(
            src_ref=ref, dst_ref=ref, send_sem=self.send.at[slot], recv_sem=self.recv.at[slot],
            device_id=place(self.here, 1 - self.core), device_id_type=pl.DeviceIdType.MESH).wait_recv()

    def shifted(self, dim, j):
        return {**self.here, dim: (self.here[dim] + j + 4) % 4}

    def group(self, depth, chip):
        return {**chip, **{d: ALL for d in self.order[:depth]}}

    def half(self, chip, k):
        dim = [d for d in self.order[:2] if d != "y"][0]
        return {**self.group(2, chip), dim: pl.ds(2 * k, 2)}

    def ring(self, depth):
        dim = self.order[depth]
        for j in (1, 3, 2):
            self.copy(self.group(depth, self.here), 3 * depth + j - 1, self.shifted(dim, j), self.core).start()

    def ring_landed(self, depth):
        dim = self.order[depth]
        for j in (1, 3, 2):
            self.landed(self.group(depth, self.shifted(dim, -j)), 3 * depth + j - 1)

    def last(self):
        dim = self.order[2]
        right, left = self.shifted(dim, 1), self.shifted(dim, -1)
        self.copy(self.half(self.here, 0), 6, right, self.core).start()
        self.copy(self.half(self.here, 1), 7, left, self.core).start()
        self.copy(self.half(self.here, 1), 8, right, self.core).start()
        self.copy(self.half(self.here, 0), 9, left, self.core).start()
        self.other(self.here, 12)

    def other(self, chip, slot):
        self.copy(self.group(2, chip), slot, self.here, 1 - self.core).start()

    def forward(self):
        dim = self.order[2]
        right, left = self.shifted(dim, 1), self.shifted(dim, -1)
        self.landed(self.half(left, 0), 6)
        self.copy(self.half(left, 0), 10, right, self.core).start()
        self.landed(self.half(right, 1), 7)
        self.copy(self.half(right, 1), 11, left, self.core).start()

    def sides(self):
        dim = self.order[2]
        right, left = self.shifted(dim, 1), self.shifted(dim, -1)
        self.landed(self.half(left, 1), 8)
        self.other(left, 13)
        self.landed(self.half(right, 0), 9)
        self.other(right, 14)

    def far(self):
        far = self.shifted(self.order[2], 2)
        self.landed(self.half(far, 0), 10)
        self.landed(self.half(far, 1), 11)
        self.other(far, 15)

    def others_landed(self):
        dim = self.order[2]
        for j, slot in ((0, 12), (-1, 13), (1, 14), (2, 15)):
            chip = self.group(2, self.shifted(dim, j))
            ref = view(self.buf, chip, 1 - self.core, self.lanes)
            pltpu.make_async_remote_copy(
                src_ref=ref, dst_ref=ref, send_sem=self.send.at[slot], recv_sem=self.recv.at[slot],
                device_id=place(self.here, 1 - self.core), device_id_type=pl.DeviceIdType.MESH).wait_recv()

    def sent(self):
        dim = self.order[2]
        right, left, far = self.shifted(dim, 1), self.shifted(dim, -1), self.shifted(dim, 2)
        for depth in (0, 1):
            for j in (1, 2, 3):
                self.copy(self.group(depth, self.here), 3 * depth + j - 1, self.shifted(self.order[depth], j), self.core).wait_send()
        for slot, chip, k, to in ((6, self.here, 0, right), (7, self.here, 1, left), (8, self.here, 1, right), (9, self.here, 0, left), (10, left, 0, right), (11, right, 1, left)):
            self.copy(self.half(chip, k), slot, to, self.core).wait_send()
        for slot, chip in ((12, self.here), (13, left), (14, right), (15, far)):
            self.copy(self.group(2, chip), slot, self.here, 1 - self.core).wait_send()


def position():
    seq, head = lax.axis_index("seq"), lax.axis_index("head")
    here = {"x": seq % 4, "y": (head // 2) * 2 + seq // 16, "z": (seq // 4) % 4}
    return here, head % 2, head


def greet(here, core):
    barrier = pltpu.get_barrier_semaphore()
    peers = [({**here, d: (here[d] + j) % 4}, core) for d in "xyz" for j in (1, 2, 3)]
    peers += [(here, 1 - core), ({**here, "y": (here["y"] + 2) % 4}, 1 - core)]
    for chip, c in peers:
        pl.semaphore_signal(barrier, inc=1, device_id=place(chip, c), device_id_type=pl.DeviceIdType.MESH)
    pl.semaphore_wait(barrier, len(peers))


def finish(mixed, gain, cos, sin):
    latent, a, b = mixed[:, :LATENT], mixed[:, LATENT : LATENT + HALF], mixed[:, LATENT + HALF :]
    normed = latent * lax.rsqrt(jnp.mean(latent * latent, axis=1, keepdims=True) + 1e-06) * gain
    return jnp.concatenate([normed, a * cos - b * sin, a * sin + b * cos], axis=1).astype(jnp.bfloat16)


def each(group, name, *args):
    for item in group:
        getattr(item, name)(*args)


def kernel(heads, toks, len_ref, tab_ref, gain_ref, tok_hbm, down_hbm, pre_hbm, qn_hbm, qr_hbm, ku_hbm, vu_hbm,
           out_ref, pool_ref, pbuf, nbuf, part, parts, tok_ref, down_ref, qn_ref, qr_ref, ku_ref, vu_ref,
           qt, acc, m_s, l_s, sb, vt, in_sem, send, recv, rs_send, rs_recv):
    here, core, head = position()
    seq = lax.axis_index("seq")
    rows, prow = nbuf.shape[5], pbuf.shape[5]
    mine = (here["y"] % 2, here["z"], here["x"], here["y"] // 2, core)
    loads = [pltpu.make_async_copy(src, dst, in_sem.at[i]) for i, (src, dst) in enumerate((
        (pre_hbm.at[pl.ds(head * prow, prow), :], pbuf.at[mine]), (tok_hbm, tok_ref), (down_hbm, down_ref),
        (qn_hbm, qn_ref), (ku_hbm, ku_ref), (qr_hbm, qr_ref), (vu_hbm, vu_ref)))]
    for load in loads:
        load.start()
    greet(here, core)
    loads[0].wait()
    pre = [Spread(pbuf, LANES[i], ORDERS[i], here, core, send.at[i], recv.at[i]) for i in range(3)]
    new = [Spread(nbuf, LANES[i], ORDERS[(i + 1) % 3], here, core, send.at[3 + i], recv.at[3 + i]) for i in range(3)]
    each(pre, "ring", 0)

    loads[1].wait()
    loads[2].wait()
    term = lax.dot_general(tok_ref[...], down_ref[...], (((1,), (1,)), ((), ())), preferred_element_type=jnp.float32)
    part[...] = term.astype(jnp.bfloat16)

    def share(j):
        to = (head + j) % 4
        return pltpu.make_async_remote_copy(
            src_ref=part.at[pl.ds(to * rows, rows), :], dst_ref=parts.at[j - 1], send_sem=rs_send.at[j - 1], recv_sem=rs_recv.at[j - 1],
            device_id={"seq": seq, "head": to}, device_id_type=pl.DeviceIdType.MESH)

    for j in (1, 2, 3):
        share(j).start()
    each(pre, "ring_landed", 0)
    each(pre, "ring", 1)
    turn = tab_ref[...].T
    for j in (1, 2, 3):
        share(j).wait_recv()
    own_rows = pl.ds(pl.multiple_of(head * rows, rows), rows)
    mixed = part[own_rows, :].astype(jnp.float32)
    for j in range(3):
        mixed += parts[j].astype(jnp.float32)
    nbuf[mine] = finish(mixed, gain_ref[...], tab_ref[own_rows, :HALF], tab_ref[own_rows, HALF : 2 * HALF])
    each(new, "ring", 0)

    def lift(h):
        cols = pl.ds(h * toks, toks)
        lifted = jnp.dot(qn_ref[:, pl.ds(h * NOPE, NOPE)], ku_ref[h], preferred_element_type=jnp.float32)
        qt[:LATENT, cols] = lifted.T.astype(jnp.bfloat16)

    def rotate(g):
        cos, sin = turn[:HALF], turn[HALF : 2 * HALF]
        both = qr_ref[:, pl.ds(g * 2 * ROPE, 2 * ROPE)].astype(jnp.float32).T
        for e in range(2):
            a, b = both[ROPE * e : ROPE * e + HALF], both[ROPE * e + HALF : ROPE * (e + 1)]
            cols = pl.ds((2 * g + e) * toks, toks)
            qt[LATENT : LATENT + HALF, cols] = (a * cos - b * sin).astype(jnp.bfloat16)
            qt[LATENT + HALF :, cols] = (a * sin + b * cos).astype(jnp.bfloat16)

    loads[3].wait()
    loads[4].wait()
    for h in range(heads // 2):
        lift(h)
    each(pre, "ring_landed", 1)
    each(pre, "last")
    each(new, "ring_landed", 0)
    each(new, "ring", 1)
    for h in range(heads // 2, heads):
        lift(h)
    loads[5].wait()
    each(pre, "forward")
    for g in range(heads // 2):
        rotate(g)
    m_s[...] = jnp.full_like(m_s, NEG)
    l_s[...] = jnp.zeros_like(l_s)
    acc[...] = jnp.zeros_like(acc)
    each(new, "ring_landed", 1)
    each(new, "last")
    each(pre, "sides")
    each(pre, "far")
    each(pre, "others_landed")

    first_row = seq * toks
    own_blocks = (first_row + toks + KB - 1) // KB
    pre_blocks = pbuf.size // (WIDTH * KB)

    def pre_keys(b):
        return pbuf[b // 2, pl.ds(2 * (b % 2), 2)].reshape(KB, WIDTH)

    def new_keys(b):
        return nbuf[b // 4, b % 4].reshape(KB, WIDTH)

    def score(keys, slot):
        sb[slot] = jnp.dot(keys, qt[...], preferred_element_type=jnp.float32)

    def hide(slot, limit, step):
        for h in range(heads):
            cols = pl.ds(h * toks, toks)
            key = lax.broadcasted_iota(jnp.int32, (KB, toks), 0)
            tok = lax.broadcasted_iota(jnp.int32, (KB, toks), 1)
            sb[slot, :, cols] = jnp.where(key <= tok * step + limit, sb[slot, :, cols], NEG)

    def score_new(b, slot):
        score(new_keys(b), slot)
        @pl.when(b == own_blocks - 1)
        def _():
            hide(slot, first_row - b * KB, 1)

    def score_pre(b, slot):
        score(pre_keys(b), slot)
        if b >= 2:
            hide(slot, len_ref[0] - b * KB - 1, 0)

    def soft(keys, slot):
        vt[...] = keys[:, :LATENT].T
        s = sb[slot]
        old = m_s[0:1]
        top = jnp.maximum(old, jnp.max(s, axis=0, keepdims=True))
        fade = jnp.exp2((old - top) * SCALE)
        m_s[0:1] = top
        w = jnp.exp2((s - top) * SCALE)
        l_s[0:1] = l_s[0:1] * fade + jnp.sum(w, axis=0, keepdims=True)
        acc[...] = acc[...] * fade + jnp.dot(vt[...], w.astype(jnp.bfloat16), preferred_element_type=jnp.float32)

    score_pre(0, 0)
    score_pre(1, 1)
    soft(pre_keys(0), 0)
    each(new, "forward")
    score_pre(2, 0)
    soft(pre_keys(1), 1)
    each(new, "sides")
    score_pre(3, 1)
    soft(pre_keys(2), 0)
    each(new, "far")
    each(new, "others_landed")
    score_new(0, 0)
    soft(pre_keys(3), 1)

    def step(pair, carry):
        for u in range(2):
            b = pair * 2 + u
            @pl.when(b < own_blocks)
            def _():
                score_new(jnp.minimum(b + 1, own_blocks - 1), 1 - u)
                soft(new_keys(b), u)
        return carry

    lax.fori_loop(0, (own_blocks + 1) // 2, step, 0)

    wanted = tab_ref[:, 2 * HALF : 2 * HALF + 1]
    picked = jnp.zeros((toks, WIDTH), jnp.float32)
    for b in range(nbuf.size // (WIDTH * KB)):
        row = lax.broadcasted_iota(jnp.int32, (toks, KB), 1).astype(jnp.float32) + float(b * KB)
        pick = jnp.where(row == wanted, 1.0, 0.0).astype(jnp.bfloat16)
        picked += jnp.dot(pick, new_keys(b), preferred_element_type=jnp.float32)
    pool_ref[...] = picked.astype(jnp.bfloat16)
    loads[6].wait()
    for h in range(heads):
        cols = pl.ds(h * toks, toks)
        att = (acc[:, cols] / l_s[0:1, cols]).astype(jnp.bfloat16)
        out_ref[:, pl.ds(h * VHEAD, VHEAD)] = lax.dot_general(att, vu_ref[h], (((0,), (0,)), ((), ())), preferred_element_type=jnp.float32).astype(jnp.bfloat16)
    each(pre, "sent")
    each(new, "sent")
    for j in (1, 2, 3):
        share(j).wait_send()


def per_device(tokens, latent_down, latent_gain, query_nope, query_rope, key_up, value_up, prefix_latent, prefix_length, page_table):
    toks, heads = tokens.shape[0], key_up.shape[0]
    seq = lax.axis_index("seq")
    positions = prefix_length[0] + seq * toks + jnp.arange(toks, dtype=jnp.int32)
    frequency = 10000.0 ** (-jnp.arange(HALF, dtype=jnp.float32) / HALF)
    angle = positions.astype(jnp.float32)[:, None] * frequency[None, :]
    pages = toks // PAGE
    slots = seq * pages + jnp.arange(toks, dtype=jnp.int32) // PAGE
    count = page_table.shape[0]
    page = jnp.sum(jnp.where(page_table[None, :] == slots[:, None], jnp.arange(count, dtype=jnp.int32)[None, :], 0), axis=1)
    row = (page * PAGE + jnp.arange(toks, dtype=jnp.int32) % PAGE).astype(jnp.float32)
    table = jnp.concatenate([jnp.cos(angle), jnp.sin(angle), jnp.broadcast_to(row[:, None], (toks, 2 * HALF))], axis=1)
    rows, prow = toks // 4, prefix_latent.shape[0] // 4
    grid = (2, 4, 4, 2, 2)
    queries = heads * toks
    vm, sm, hbm = (pl.BlockSpec(memory_space=m) for m in (pltpu.VMEM, pltpu.SMEM, pl.ANY))
    bf, f32, dma = jnp.bfloat16, jnp.float32, pltpu.SemaphoreType.DMA
    down = latent_down.T
    attended, pool = pl.pallas_call(
        functools.partial(kernel, heads, toks),
        out_shape=[jax.ShapeDtypeStruct((toks, heads * VHEAD), bf), jax.ShapeDtypeStruct((toks, WIDTH), bf)],
        in_specs=[sm, vm, vm] + [hbm] * 7, out_specs=[vm, vm],
        scratch_shapes=[
            pltpu.VMEM((*grid, prow, WIDTH), bf), pltpu.VMEM((*grid, rows, WIDTH), bf),
            pltpu.VMEM((toks, WIDTH), bf), pltpu.VMEM((3, rows, WIDTH), bf),
            pltpu.VMEM(tokens.shape, bf), pltpu.VMEM(down.shape, bf),
            pltpu.VMEM(query_nope.shape, bf), pltpu.VMEM(query_rope.shape, bf), pltpu.VMEM(key_up.shape, bf), pltpu.VMEM(value_up.shape, bf),
            pltpu.VMEM((WIDTH, queries), bf), pltpu.VMEM((LATENT, queries), f32), pltpu.VMEM((8, queries), f32), pltpu.VMEM((8, queries), f32),
            pltpu.VMEM((2, KB, queries), f32), pltpu.VMEM((LATENT, KB), bf),
            dma((7,)), dma((6, 16)), dma((6, 16)), dma((3,)), dma((3,))],
        compiler_params=pltpu.CompilerParams(vmem_limit_bytes=63 << 20, collective_id=0, has_side_effects=True), name="latent_attention",
    )(prefix_length, table, latent_gain.reshape(1, LATENT), tokens, down, prefix_latent, query_nope, query_rope, key_up, value_up)
    return attended, pool.reshape(pages, PAGE * WIDTH)


def solution(mesh):
    placed = (P("seq", "head"), P("head", None), P(), P("seq", "head"), P("seq", "head"), P("head", None, None), P("head", None, None), P("seq", None), P(), P())
    return jax.shard_map(per_device, mesh=mesh, in_specs=placed, out_specs=(P("seq", "head"), P("seq", None)), check_vma=False)
```

```python
import functools
import jax
import jax.numpy as jnp
from jax import lax
from jax.experimental import pallas as pl
from jax.experimental.pallas import tpu as pltpu
from jax.sharding import PartitionSpec as P
LATENT, ROPE, NOPE, VHEAD, PAGE = 512, 64, 128, 128, 16
WIDTH = LATENT + ROPE
HALF = ROPE // 2
PADDED = 640
KB = 512
SCALE = (NOPE + ROPE) ** -0.5 * 1.4426950408889634
NEG = -1e30
ORDERS = (("x", "y", "z"), ("y", "z", "x"), ("z", "x", "y"))
LANES = (pl.ds(0, 256), pl.ds(256, 256), pl.ds(512, 128))
ALL = slice(None)


def place(chip, core):
    y_hi, y_lo = chip["y"] // 2, chip["y"] % 2
    return {"seq": y_lo * 16 + chip["z"] * 4 + chip["x"], "head": y_hi * 2 + core}


def view(buf, chip, core, lanes):
    y = chip["y"]
    y_lo, y_hi = (ALL, ALL) if isinstance(y, slice) else (y % 2, y // 2)
    return buf.at[y_lo, chip["z"], chip["x"], y_hi, core, :, lanes]


class Spread:
    def __init__(self, buf, lanes, order, here, core, send, recv):
        self.buf, self.lanes, self.order = buf, lanes, order
        self.here, self.core, self.send, self.recv = here, core, send, recv

    def copy(self, chip, slot, to, core):
        ref = view(self.buf, chip, self.core, self.lanes)
        return pltpu.make_async_remote_copy(
            src_ref=ref, dst_ref=ref, send_sem=self.send.at[slot], recv_sem=self.recv.at[slot],
            device_id=place(to, core), device_id_type=pl.DeviceIdType.MESH)

    def landed(self, chip, slot):
        ref = view(self.buf, chip, self.core, self.lanes)
        pltpu.make_async_remote_copy(
            src_ref=ref, dst_ref=ref, send_sem=self.send.at[slot], recv_sem=self.recv.at[slot],
            device_id=place(self.here, 1 - self.core), device_id_type=pl.DeviceIdType.MESH).wait_recv()

    def shifted(self, dim, j):
        return {**self.here, dim: (self.here[dim] + j + 4) % 4}

    def group(self, depth, chip):
        return {**chip, **{d: ALL for d in self.order[:depth]}}

    def half(self, chip, k):
        dim = [d for d in self.order[:2] if d != "y"][0]
        return {**self.group(2, chip), dim: pl.ds(2 * k, 2)}

    def ring(self, depth):
        dim = self.order[depth]
        for j in (1, 3, 2):
            self.copy(self.group(depth, self.here), 3 * depth + j - 1, self.shifted(dim, j), self.core).start()

    def ring_landed(self, depth):
        dim = self.order[depth]
        for j in (1, 3, 2):
            self.landed(self.group(depth, self.shifted(dim, -j)), 3 * depth + j - 1)

    def last(self):
        dim = self.order[2]
        right, left = self.shifted(dim, 1), self.shifted(dim, -1)
        self.copy(self.half(self.here, 0), 6, right, self.core).start()
        self.copy(self.half(self.here, 1), 7, left, self.core).start()
        self.copy(self.half(self.here, 1), 8, right, self.core).start()
        self.copy(self.half(self.here, 0), 9, left, self.core).start()
        self.other(self.here, 12)

    def other(self, chip, slot):
        self.copy(self.group(2, chip), slot, self.here, 1 - self.core).start()

    def forward(self):
        dim = self.order[2]
        right, left = self.shifted(dim, 1), self.shifted(dim, -1)
        self.landed(self.half(left, 0), 6)
        self.copy(self.half(left, 0), 10, right, self.core).start()
        self.landed(self.half(right, 1), 7)
        self.copy(self.half(right, 1), 11, left, self.core).start()

    def sides(self):
        dim = self.order[2]
        right, left = self.shifted(dim, 1), self.shifted(dim, -1)
        self.landed(self.half(left, 1), 8)
        self.other(left, 13)
        self.landed(self.half(right, 0), 9)
        self.other(right, 14)

    def far(self):
        far = self.shifted(self.order[2], 2)
        self.landed(self.half(far, 0), 10)
        self.landed(self.half(far, 1), 11)
        self.other(far, 15)

    def others_landed(self):
        dim = self.order[2]
        for j, slot in ((0, 12), (-1, 13), (1, 14), (2, 15)):
            chip = self.group(2, self.shifted(dim, j))
            ref = view(self.buf, chip, 1 - self.core, self.lanes)
            pltpu.make_async_remote_copy(
                src_ref=ref, dst_ref=ref, send_sem=self.send.at[slot], recv_sem=self.recv.at[slot],
                device_id=place(self.here, 1 - self.core), device_id_type=pl.DeviceIdType.MESH).wait_recv()

    def sent(self):
        dim = self.order[2]
        right, left, far = self.shifted(dim, 1), self.shifted(dim, -1), self.shifted(dim, 2)
        for depth in (0, 1):
            for j in (1, 2, 3):
                self.copy(self.group(depth, self.here), 3 * depth + j - 1, self.shifted(self.order[depth], j), self.core).wait_send()
        for slot, chip, k, to in ((6, self.here, 0, right), (7, self.here, 1, left), (8, self.here, 1, right), (9, self.here, 0, left), (10, left, 0, right), (11, right, 1, left)):
            self.copy(self.half(chip, k), slot, to, self.core).wait_send()
        for slot, chip in ((12, self.here), (13, left), (14, right), (15, far)):
            self.copy(self.group(2, chip), slot, self.here, 1 - self.core).wait_send()


PLANES = (("z", "x", "y"), ("x", "y", "z"))


class Plane(Spread):
    def __init__(self, buf, here, core, send, recv):
        super().__init__(buf, ALL, PLANES[core], here, core, send, recv)

    def near(self, i, j):
        a, b, _ = self.order
        return {**self.here, a: (self.here[a] + i + 4) % 4, b: (self.here[b] + j + 4) % 4}

    def spots(self):
        return [(i, j) for i in (1, 3, 0, 2) for j in (1, 3, 0, 2) if i or j]

    def plane(self):
        for i, j in self.spots():
            self.copy(self.here, 4 * i + j, self.near(i, j), self.core).start()

    def plane_landed(self):
        for i, j in self.spots():
            self.landed(self.near(-i, -j), 4 * i + j)

    def across(self):
        for j in (1, 3, 2):
            self.copy(self.group(2, self.here), 15 + j, self.shifted(self.order[2], j), self.core).start()
        self.other(self.here, 19)

    def across_landed(self, k):
        chip = self.shifted(self.order[2], k)
        self.landed(self.group(2, chip), 15 + (4 - k) % 4)
        self.other(chip, 19 + k)

    def block_landed(self, k):
        twin = Plane(self.buf, self.here, 1 - self.core, self.send, self.recv)
        twin.landed(twin.group(2, twin.shifted(twin.order[2], k)), 19 + k)

    def all_sent(self):
        for i, j in self.spots():
            self.copy(self.here, 4 * i + j, self.near(i, j), self.core).wait_send()
        for j in (1, 2, 3):
            self.copy(self.group(2, self.here), 15 + j, self.shifted(self.order[2], j), self.core).wait_send()
        for k in range(4):
            self.copy(self.group(2, self.shifted(self.order[2], k)), 19 + k, self.here, 1 - self.core).wait_send()


def position():
    seq, head = lax.axis_index("seq"), lax.axis_index("head")
    here = {"x": seq % 4, "y": (head // 2) * 2 + seq // 16, "z": (seq // 4) % 4}
    return here, head % 2, head


def greet(here, core):
    barrier = pltpu.get_barrier_semaphore()

    def signal(chip, c):
        pl.semaphore_signal(barrier, inc=1, device_id=place(chip, c), device_id_type=pl.DeviceIdType.MESH)

    for d in "xyz":
        for j in (1, 2, 3):
            signal({**here, d: (here[d] + j) % 4}, core)
    signal(here, 1 - core)
    signal({**here, "y": (here["y"] + 2) % 4}, 1 - core)
    for c in range(2):
        @pl.when(core == c)
        def _():
            a, b, _ = PLANES[c]
            for i in (1, 2, 3):
                for j in (1, 2, 3):
                    signal({**here, a: (here[a] + i) % 4, b: (here[b] + j) % 4}, c)


def greeted():
    pl.semaphore_wait(pltpu.get_barrier_semaphore(), 20)


def finish(mixed, gain, cos, sin):
    latent, a, b = mixed[:, :LATENT], mixed[:, LATENT : LATENT + HALF], mixed[:, LATENT + HALF : WIDTH]
    normed = latent * lax.rsqrt(jnp.mean(latent * latent, axis=1, keepdims=True) + 1e-06) * gain
    spare = jnp.zeros((mixed.shape[0], PADDED - WIDTH), jnp.float32)
    return jnp.concatenate([normed, a * cos - b * sin, a * sin + b * cos, spare], axis=1).astype(jnp.bfloat16)


def each(group, name, *args):
    for item in group:
        getattr(item, name)(*args)


def kernel(heads, toks, len_ref, tab_ref, gain_ref, tok_hbm, down_hbm, pre_hbm, qn_hbm, qr_hbm, ku_hbm, vu_hbm,
           out_ref, pool_ref, pbuf, nbuf, pown, part, parts, tok_ref, down_ref, qn_ref, qr_ref, ku_ref, vu_ref,
           qt, acc, m_s, l_s, sb, vt, in_sem, pre_send, pre_recv, send, recv, rs_send, rs_recv):
    here, core, head = position()
    seq = lax.axis_index("seq")
    rows, prow = nbuf.shape[5], pbuf.shape[5]
    mine = (here["y"] % 2, here["z"], here["x"], here["y"] // 2, core)
    loads = [pltpu.make_async_copy(src, dst, in_sem.at[i]) for i, (src, dst) in enumerate((
        (tok_hbm, tok_ref), (down_hbm, down_ref), (pre_hbm.at[pl.ds(head * prow, prow), :], pown),
        (qn_hbm, qn_ref), (ku_hbm, ku_ref), (qr_hbm, qr_ref), (vu_hbm, vu_ref)))]
    for load in loads:
        load.start()
    greet(here, core)
    new = [Spread(nbuf, LANES[i], ORDERS[(i + 1) % 3], here, core, send.at[i], recv.at[i]) for i in range(3)]

    def prefix(name, *args):
        for c in range(2):
            @pl.when(core == c)
            def _():
                getattr(Plane(pbuf, here, c, pre_send, pre_recv), name)(*args)


    loads[0].wait()
    loads[1].wait()
    term = lax.dot_general(tok_ref[...], down_ref[...], (((1,), (1,)), ((), ())), preferred_element_type=jnp.float32)
    part[...] = term.astype(jnp.bfloat16)

    def share(j):
        to = (head + j) % 4
        return pltpu.make_async_remote_copy(
            src_ref=part.at[pl.ds(to * rows, rows), :], dst_ref=parts.at[j - 1], send_sem=rs_send.at[j - 1], recv_sem=rs_recv.at[j - 1],
            device_id={"seq": seq, "head": to}, device_id_type=pl.DeviceIdType.MESH)

    def lift(h):
        cols = pl.ds(h * toks, toks)
        lifted = jnp.dot(qn_ref[:, pl.ds(h * NOPE, NOPE)], ku_ref[h], preferred_element_type=jnp.float32)
        qt[:LATENT, cols] = lifted.T.astype(jnp.bfloat16)

    turn = tab_ref[...].T

    def rotate(g):
        cos, sin = turn[:HALF], turn[HALF : 2 * HALF]
        both = qr_ref[:, pl.ds(g * 2 * ROPE, 2 * ROPE)].astype(jnp.float32).T
        for e in range(2):
            a, b = both[ROPE * e : ROPE * e + HALF], both[ROPE * e + HALF : ROPE * (e + 1)]
            cols = pl.ds((2 * g + e) * toks, toks)
            qt[LATENT : LATENT + HALF, cols] = (a * cos - b * sin).astype(jnp.bfloat16)
            qt[LATENT + HALF : WIDTH, cols] = (a * sin + b * cos).astype(jnp.bfloat16)

    loads[2].wait()
    spare = (prow, PADDED - WIDTH)
    row = seq * 4 * prow + head * prow + lax.broadcasted_iota(jnp.int32, spare, 0)
    dead = (row >= len_ref[0]) & (lax.broadcasted_iota(jnp.int32, spare, 1) == 0)
    pbuf[mine] = jnp.concatenate([pown[...], jnp.where(dead, NEG, 0.0).astype(jnp.bfloat16)], axis=1)
    loads[3].wait()
    loads[4].wait()
    for h in range(heads // 2):
        lift(h)
    greeted()
    for j in (1, 2, 3):
        share(j).start()
    prefix("plane")
    for h in range(heads // 2, heads):
        lift(h)
    for j in (1, 2, 3):
        share(j).wait_recv()
    own_rows = pl.ds(pl.multiple_of(head * rows, rows), rows)
    mixed = part[own_rows, :].astype(jnp.float32)
    for j in range(3):
        mixed += parts[j].astype(jnp.float32)
    nbuf[mine] = finish(mixed, gain_ref[...], tab_ref[own_rows, :HALF], tab_ref[own_rows, HALF : 2 * HALF])
    each(new, "ring", 0)
    prefix("plane_landed")
    prefix("across")
    loads[5].wait()
    for g in range(heads // 2):
        rotate(g)
    ones = lax.broadcasted_iota(jnp.int32, (PADDED - WIDTH, heads * toks), 0) == 0
    qt[WIDTH:, :] = jnp.where(ones, 1.0, 0.0).astype(jnp.bfloat16)
    m_s[...] = jnp.full_like(m_s, NEG)
    l_s[...] = jnp.zeros_like(l_s)
    acc[...] = jnp.zeros_like(acc)

    first_row = seq * toks
    own_blocks = (first_row + toks + KB - 1) // KB

    def pre_keys(k):
        y, z = (here["y"] + k) % 4, (here["z"] + k) % 4
        even = pbuf[y % 2, :, :, y // 2, 0].reshape(KB // 2, PADDED)
        odd = pbuf[:, z, :, :, 1].reshape(KB // 2, PADDED)
        return jnp.concatenate([even, odd], axis=0)

    def new_keys(b):
        return nbuf[b // 4, b % 4].reshape(KB, PADDED)

    def score(keys, slot):
        sb[slot] = jnp.dot(keys, qt[...], preferred_element_type=jnp.float32)

    def hide(slot, limit, step):
        for h in range(heads):
            cols = pl.ds(h * toks, toks)
            key = lax.broadcasted_iota(jnp.int32, (KB, toks), 0)
            tok = lax.broadcasted_iota(jnp.int32, (KB, toks), 1)
            sb[slot, :, cols] = jnp.where(key <= tok * step + limit, sb[slot, :, cols], NEG)

    def score_new(b, slot):
        score(new_keys(b), slot)
        @pl.when(b == own_blocks - 1)
        def _():
            hide(slot, first_row - b * KB, 1)

    def score_pre(k, slot):
        prefix("block_landed", k)
        score(pre_keys(k), slot)

    def soft(keys, slot):
        vt[...] = keys[:, :LATENT].T
        s = sb[slot]
        old = m_s[0:1]
        top = jnp.maximum(old, jnp.max(s, axis=0, keepdims=True))
        fade = jnp.exp2((old - top) * SCALE)
        m_s[0:1] = top
        w = jnp.exp2((s - top) * SCALE)
        l_s[0:1] = l_s[0:1] * fade + jnp.sum(w, axis=0, keepdims=True)
        acc[...] = acc[...] * fade + jnp.dot(vt[...], w.astype(jnp.bfloat16), preferred_element_type=jnp.float32)

    score_pre(0, 0)
    each(new, "ring_landed", 0)
    each(new, "ring", 1)
    prefix("across_landed", 1)
    prefix("across_landed", 3)
    score_pre(1, 1)
    soft(pre_keys(0), 0)
    each(new, "ring_landed", 1)
    each(new, "last")
    prefix("across_landed", 2)
    score_pre(3, 0)
    soft(pre_keys(1), 1)
    each(new, "forward")
    score_pre(2, 1)
    soft(pre_keys(3), 0)
    each(new, "sides")
    each(new, "far")
    each(new, "others_landed")
    score_new(0, 0)
    soft(pre_keys(2), 1)

    def step(pair, carry):
        for u in range(2):
            b = pair * 2 + u
            @pl.when(b < own_blocks)
            def _():
                score_new(jnp.minimum(b + 1, own_blocks - 1), 1 - u)
                soft(new_keys(b), u)
        return carry

    lax.fori_loop(0, (own_blocks + 1) // 2, step, 0)

    wanted = tab_ref[:, 2 * HALF : 2 * HALF + 1]
    picked = jnp.zeros((toks, WIDTH), jnp.float32)
    for b in range(nbuf.size // (PADDED * KB)):
        row = lax.broadcasted_iota(jnp.int32, (toks, KB), 1).astype(jnp.float32) + float(b * KB)
        pick = jnp.where(row == wanted, 1.0, 0.0).astype(jnp.bfloat16)
        picked += jnp.dot(pick, new_keys(b)[:, :WIDTH], preferred_element_type=jnp.float32)
    pool_ref[...] = picked.astype(jnp.bfloat16)
    loads[6].wait()
    for h in range(heads):
        cols = pl.ds(h * toks, toks)
        att = (acc[:, cols] / l_s[0:1, cols]).astype(jnp.bfloat16)
        out_ref[:, pl.ds(h * VHEAD, VHEAD)] = lax.dot_general(att, vu_ref[h], (((0,), (0,)), ((), ())), preferred_element_type=jnp.float32).astype(jnp.bfloat16)
    prefix("all_sent")
    each(new, "sent")
    for j in (1, 2, 3):
        share(j).wait_send()


def per_device(tokens, latent_down, latent_gain, query_nope, query_rope, key_up, value_up, prefix_latent, prefix_length, page_table):
    toks, heads = tokens.shape[0], key_up.shape[0]
    seq = lax.axis_index("seq")
    positions = prefix_length[0] + seq * toks + jnp.arange(toks, dtype=jnp.int32)
    frequency = 10000.0 ** (-jnp.arange(HALF, dtype=jnp.float32) / HALF)
    angle = positions.astype(jnp.float32)[:, None] * frequency[None, :]
    pages = toks // PAGE
    slots = seq * pages + jnp.arange(toks, dtype=jnp.int32) // PAGE
    count = page_table.shape[0]
    page = jnp.sum(jnp.where(page_table[None, :] == slots[:, None], jnp.arange(count, dtype=jnp.int32)[None, :], 0), axis=1)
    row = (page * PAGE + jnp.arange(toks, dtype=jnp.int32) % PAGE).astype(jnp.float32)
    table = jnp.concatenate([jnp.cos(angle), jnp.sin(angle), jnp.broadcast_to(row[:, None], (toks, 2 * HALF))], axis=1)
    rows, prow = toks // 4, prefix_latent.shape[0] // 4
    grid = (2, 4, 4, 2, 2)
    queries = heads * toks
    vm, sm, hbm = (pl.BlockSpec(memory_space=m) for m in (pltpu.VMEM, pltpu.SMEM, pl.ANY))
    bf, f32, dma = jnp.bfloat16, jnp.float32, pltpu.SemaphoreType.DMA
    down = latent_down.T
    attended, pool = pl.pallas_call(
        functools.partial(kernel, heads, toks),
        out_shape=[jax.ShapeDtypeStruct((toks, heads * VHEAD), bf), jax.ShapeDtypeStruct((toks, WIDTH), bf)],
        in_specs=[sm, vm, vm] + [hbm] * 7, out_specs=[vm, vm],
        scratch_shapes=[
            pltpu.VMEM((*grid, prow, PADDED), bf), pltpu.VMEM((*grid, rows, PADDED), bf),
            pltpu.VMEM((prow, WIDTH), bf), pltpu.VMEM((toks, WIDTH), bf), pltpu.VMEM((3, rows, WIDTH), bf),
            pltpu.VMEM(tokens.shape, bf), pltpu.VMEM(down.shape, bf),
            pltpu.VMEM(query_nope.shape, bf), pltpu.VMEM(query_rope.shape, bf), pltpu.VMEM(key_up.shape, bf), pltpu.VMEM(value_up.shape, bf),
            pltpu.VMEM((PADDED, queries), bf), pltpu.VMEM((LATENT, queries), f32), pltpu.VMEM((8, queries), f32), pltpu.VMEM((8, queries), f32),
            pltpu.VMEM((2, KB, queries), f32), pltpu.VMEM((LATENT, KB), bf),
            dma((7,)), dma((23,)), dma((23,)), dma((3, 16)), dma((3, 16)), dma((3,)), dma((3,))],
        compiler_params=pltpu.CompilerParams(vmem_limit_bytes=63 << 20, collective_id=0, has_side_effects=True), name="latent_attention",
    )(prefix_length, table, latent_gain.reshape(1, LATENT), tokens, down, prefix_latent, query_nope, query_rope, key_up, value_up)
    return attended, pool.reshape(pages, PAGE * WIDTH)


def solution(mesh):
    placed = (P("seq", "head"), P("head", None), P(), P("seq", "head"), P("seq", "head"), P("head", None, None), P("head", None, None), P("seq", None), P(), P())
    return jax.shard_map(per_device, mesh=mesh, in_specs=placed, out_specs=(P("seq", "head"), P("seq", None)), check_vma=False)
```

```python
import functools
import jax
import jax.numpy as jnp
from jax import lax
from jax.experimental import pallas as pl
from jax.experimental.pallas import tpu as pltpu
from jax.sharding import PartitionSpec as P
LATENT, ROPE, NOPE, VHEAD, PAGE = 512, 64, 128, 128, 16
WIDTH = LATENT + ROPE
HALF = ROPE // 2
PADDED = 640
KB = 512
SCALE = (NOPE + ROPE) ** -0.5 * 1.4426950408889634
NEG = -1e30
ALL = slice(None)


def place(chip, core):
    y_hi, y_lo = chip["y"] // 2, chip["y"] % 2
    return {"seq": y_lo * 16 + chip["z"] * 4 + chip["x"], "head": y_hi * 2 + core}


def view(buf, chip, core, lanes):
    y = chip["y"]
    y_lo, y_hi = (ALL, ALL) if isinstance(y, slice) else (y % 2, y // 2)
    return buf.at[y_lo, chip["z"], chip["x"], y_hi, core, :, lanes]


class Spread:
    cross = 5

    def __init__(self, buf, lanes, order, here, core, send, recv):
        self.buf, self.lanes, self.order = buf, lanes, order
        self.here, self.core, self.send, self.recv = here, core, send, recv

    def copy(self, chip, slot, to, core):
        ref = view(self.buf, chip, self.core, self.lanes)
        return pltpu.make_async_remote_copy(
            src_ref=ref, dst_ref=ref, send_sem=self.send.at[slot], recv_sem=self.recv.at[slot],
            device_id=place(to, core), device_id_type=pl.DeviceIdType.MESH)

    def landed(self, chip, slot):
        ref = view(self.buf, chip, self.core, self.lanes)
        pltpu.make_async_remote_copy(
            src_ref=ref, dst_ref=ref, send_sem=self.send.at[slot], recv_sem=self.recv.at[slot],
            device_id=place(self.here, 1 - self.core), device_id_type=pl.DeviceIdType.MESH).wait_recv()

    def shifted(self, dim, j):
        return {**self.here, dim: (self.here[dim] + j + 4) % 4}

    def group(self, depth, chip):
        return {**chip, **{d: ALL for d in self.order[:depth]}}

    def ring(self, depth):
        dim = self.order[depth]
        for j in (1, 3, 2):
            self.copy(self.group(depth, self.here), 3 * depth + j - 1, self.shifted(dim, j), self.core).start()

    def ring_landed(self, depth):
        dim = self.order[depth]
        for j in (1, 3, 2):
            self.landed(self.group(depth, self.shifted(dim, -j)), 3 * depth + j - 1)

    def other(self, chip, slot):
        self.copy(self.group(2, chip), slot, self.here, 1 - self.core).start()

    def across(self):
        for j in (1, 3, 2):
            self.copy(self.group(2, self.here), self.cross + j, self.shifted(self.order[2], j), self.core).start()
        self.other(self.here, self.cross + 4)

    def across_landed(self, k):
        chip = self.shifted(self.order[2], k)
        self.landed(self.group(2, chip), self.cross + (4 - k) % 4)
        self.other(chip, self.cross + 4 + k)

    def twin(self):
        return Spread(self.buf, self.lanes, self.order, self.here, 1 - self.core, self.send, self.recv)

    def block_landed(self, k):
        twin = self.twin()
        twin.landed(twin.group(2, twin.shifted(twin.order[2], k)), self.cross + 4 + k)

    def near_sent(self):
        for depth in (0, 1):
            for j in (1, 2, 3):
                self.copy(self.group(depth, self.here), 3 * depth + j - 1, self.shifted(self.order[depth], j), self.core).wait_send()

    def all_sent(self):
        self.near_sent()
        for j in (1, 2, 3):
            self.copy(self.group(2, self.here), self.cross + j, self.shifted(self.order[2], j), self.core).wait_send()
        for k in range(4):
            self.copy(self.group(2, self.shifted(self.order[2], k)), self.cross + 4 + k, self.here, 1 - self.core).wait_send()


PLANES = (("z", "x", "y"), ("x", "y", "z"))


class Plane(Spread):
    cross = 15

    def __init__(self, buf, here, core, send, recv):
        super().__init__(buf, ALL, PLANES[core], here, core, send, recv)

    def twin(self):
        return Plane(self.buf, self.here, 1 - self.core, self.send, self.recv)

    def near(self, i, j):
        a, b, _ = self.order
        return {**self.here, a: (self.here[a] + i + 4) % 4, b: (self.here[b] + j + 4) % 4}

    def spots(self):
        return [(i, j) for i in (1, 3, 0, 2) for j in (1, 3, 0, 2) if i or j]

    def plane(self):
        for i, j in self.spots():
            self.copy(self.here, 4 * i + j, self.near(i, j), self.core).start()

    def plane_landed(self):
        for i, j in self.spots():
            self.landed(self.near(-i, -j), 4 * i + j)

    def near_sent(self):
        for i, j in self.spots():
            self.copy(self.here, 4 * i + j, self.near(i, j), self.core).wait_send()


def position():
    seq, head = lax.axis_index("seq"), lax.axis_index("head")
    here = {"x": seq % 4, "y": (head // 2) * 2 + seq // 16, "z": (seq // 4) % 4}
    return here, head % 2, head


def greet(here, core):
    barrier = pltpu.get_barrier_semaphore()

    def signal(chip, c):
        pl.semaphore_signal(barrier, inc=1, device_id=place(chip, c), device_id_type=pl.DeviceIdType.MESH)

    for d in "xyz":
        for j in (1, 2, 3):
            signal({**here, d: (here[d] + j) % 4}, core)
    signal(here, 1 - core)
    signal({**here, "y": (here["y"] + 2) % 4}, 1 - core)
    for c in range(2):
        @pl.when(core == c)
        def _():
            a, b, _ = PLANES[c]
            for i in (1, 2, 3):
                for j in (1, 2, 3):
                    signal({**here, a: (here[a] + i) % 4, b: (here[b] + j) % 4}, c)


def greeted():
    pl.semaphore_wait(pltpu.get_barrier_semaphore(), 20)


def finish(mixed, gain, cos, sin):
    latent, a, b = mixed[:, :LATENT], mixed[:, LATENT : LATENT + HALF], mixed[:, LATENT + HALF : WIDTH]
    normed = latent * lax.rsqrt(jnp.mean(latent * latent, axis=1, keepdims=True) + 1e-06) * gain
    spare = jnp.zeros((mixed.shape[0], PADDED - WIDTH), jnp.float32)
    return jnp.concatenate([normed, a * cos - b * sin, a * sin + b * cos, spare], axis=1).astype(jnp.bfloat16)


def kernel(heads, toks, len_ref, tab_ref, gain_ref, tok_hbm, down_hbm, pre_hbm, qn_hbm, qr_hbm, ku_hbm, vu_hbm,
           out_ref, pool_ref, pbuf, nbuf, pown, part, parts, tok_ref, down_ref, qn_ref, qr_ref, ku_ref, vu_ref,
           qt, acc, m_s, l_s, sb, vt, in_sem, pre_send, pre_recv, send, recv, rs_send, rs_recv):
    here, core, head = position()
    seq = lax.axis_index("seq")
    rows, prow = nbuf.shape[5], pbuf.shape[5]
    mine = (here["y"] % 2, here["z"], here["x"], here["y"] // 2, core)
    loads = [pltpu.make_async_copy(src, dst, in_sem.at[i]) for i, (src, dst) in enumerate((
        (tok_hbm, tok_ref), (down_hbm, down_ref), (pre_hbm.at[pl.ds(head * prow, prow), :], pown),
        (qn_hbm, qn_ref), (ku_hbm, ku_ref), (qr_hbm, qr_ref), (vu_hbm, vu_ref)))]
    for load in loads:
        load.start()
    greet(here, core)
    def planes(buf, sends, recvs):
        def run(name, *args):
            for c in range(2):
                @pl.when(core == c)
                def _():
                    getattr(Plane(buf, here, c, sends, recvs), name)(*args)
        return run

    prefix, new = planes(pbuf, pre_send, pre_recv), planes(nbuf, send, recv)

    loads[0].wait()
    loads[1].wait()
    term = lax.dot_general(tok_ref[...], down_ref[...], (((1,), (1,)), ((), ())), preferred_element_type=jnp.float32)
    part[:, :WIDTH] = term.astype(jnp.bfloat16)
    part[:, WIDTH:] = jnp.zeros((part.shape[0], PADDED - WIDTH), jnp.bfloat16)

    def share(j):
        to = (head + j) % 4
        return pltpu.make_async_remote_copy(
            src_ref=part.at[pl.ds(to * rows, rows), :], dst_ref=parts.at[j - 1], send_sem=rs_send.at[j - 1], recv_sem=rs_recv.at[j - 1],
            device_id={"seq": seq, "head": to}, device_id_type=pl.DeviceIdType.MESH)

    def lift(h):
        cols = pl.ds(h * toks, toks)
        lifted = jnp.dot(qn_ref[:, pl.ds(h * NOPE, NOPE)], ku_ref[h], preferred_element_type=jnp.float32)
        qt[:LATENT, cols] = lifted.T.astype(jnp.bfloat16)

    turn = tab_ref[...].T

    def rotate(g):
        cos, sin = turn[:HALF], turn[HALF : 2 * HALF]
        both = qr_ref[:, pl.ds(g * 2 * ROPE, 2 * ROPE)].astype(jnp.float32).T
        for e in range(2):
            a, b = both[ROPE * e : ROPE * e + HALF], both[ROPE * e + HALF : ROPE * (e + 1)]
            cols = pl.ds((2 * g + e) * toks, toks)
            qt[LATENT : LATENT + HALF, cols] = (a * cos - b * sin).astype(jnp.bfloat16)
            qt[LATENT + HALF : WIDTH, cols] = (a * sin + b * cos).astype(jnp.bfloat16)

    loads[2].wait()
    spare = (prow, PADDED - WIDTH)
    row = seq * 4 * prow + head * prow + lax.broadcasted_iota(jnp.int32, spare, 0)
    dead = (row >= len_ref[0]) & (lax.broadcasted_iota(jnp.int32, spare, 1) == 0)
    pbuf[mine] = jnp.concatenate([pown[...], jnp.where(dead, NEG, 0.0).astype(jnp.bfloat16)], axis=1)
    loads[3].wait()
    loads[4].wait()
    for h in range(heads // 2):
        lift(h)
    greeted()
    for j in (1, 2, 3):
        share(j).start()
    prefix("plane")
    for h in range(heads // 2, heads):
        lift(h)
    for j in (1, 2, 3):
        share(j).wait_recv()
    own_rows = pl.ds(pl.multiple_of(head * rows, rows), rows)
    mixed = part[own_rows, :].astype(jnp.float32)
    for j in range(3):
        mixed += parts[j].astype(jnp.float32)
    nbuf[mine] = finish(mixed, gain_ref[...], tab_ref[own_rows, :HALF], tab_ref[own_rows, HALF : 2 * HALF])
    new("plane")
    prefix("plane_landed")
    prefix("across")
    loads[5].wait()
    for g in range(heads // 2):
        rotate(g)
    ones = lax.broadcasted_iota(jnp.int32, (PADDED - WIDTH, heads * toks), 0) == 0
    qt[WIDTH:, :] = jnp.where(ones, 1.0, 0.0).astype(jnp.bfloat16)
    m_s[...] = jnp.full_like(m_s, NEG)
    l_s[...] = jnp.zeros_like(l_s)
    acc[...] = jnp.zeros_like(acc)

    first_row = seq * toks

    def pre_keys(k):
        y, z = (here["y"] + k) % 4, (here["z"] + k) % 4
        even = pbuf[y % 2, :, :, y // 2, 0].reshape(KB // 2, PADDED)
        odd = pbuf[:, z, :, :, 1].reshape(KB // 2, PADDED)
        return jnp.concatenate([even, odd], axis=0)

    def new_keys(k, odd):
        y, z = (here["y"] + k) % 4, (here["z"] + k) % 4
        if odd:
            return nbuf[:, z, :, :, 1].reshape(KB, PADDED)
        return nbuf[y % 2, :, :, y // 2, 0].reshape(KB, PADDED)

    def place_of(k, odd):
        y, z = (here["y"] + k) % 4, (here["z"] + k) % 4
        m = lax.broadcasted_iota(jnp.int32, (KB, toks), 0)
        r, x = m % rows, m // (2 * rows if odd else rows) % 4
        if odd:
            s, h = m // (8 * rows) * 16 + z * 4 + x, m // rows % 2 * 2 + 1
            last = (19 + z * 4) * toks + toks - 1
        else:
            s, h = y % 2 * 16 + m // (4 * rows) * 4 + x, y // 2 * 2
            last = (y % 2 * 16 + 15) * toks + toks - 1
        return s * toks + h * rows + r, last

    def score(keys, slot):
        sb[slot] = jnp.dot(keys, qt[...], preferred_element_type=jnp.float32)

    def hide(k, odd):
        row, last = place_of(k, odd)

        @pl.when(last > first_row)
        def _():
            live = row <= first_row + lax.broadcasted_iota(jnp.int32, (KB, toks), 1)
            for h in range(heads):
                cols = pl.ds(h * toks, toks)
                sb[odd, :, cols] = jnp.where(live, sb[odd, :, cols], NEG)

    def score_pre(k, slot):
        prefix("block_landed", k)
        score(pre_keys(k), slot)

    def soft(keys, slot):
        vt[...] = keys[:, :LATENT].T
        s = sb[slot]
        old = m_s[0:1]
        top = jnp.maximum(old, jnp.max(s, axis=0, keepdims=True))
        fade = jnp.exp2((old - top) * SCALE)
        m_s[0:1] = top
        w = jnp.exp2((s - top) * SCALE)
        l_s[0:1] = l_s[0:1] * fade + jnp.sum(w, axis=0, keepdims=True)
        acc[...] = acc[...] * fade + jnp.dot(vt[...], w.astype(jnp.bfloat16), preferred_element_type=jnp.float32)

    score_pre(0, 0)
    new("plane_landed")
    new("across")
    soft(pre_keys(0), 0)
    prefix("across_landed", 1)
    prefix("across_landed", 3)
    score_pre(1, 1)
    prefix("across_landed", 2)
    prefix("block_landed", 3)
    score(pre_keys(3), 0)
    soft(pre_keys(1), 1)
    prefix("block_landed", 2)
    score(pre_keys(2), 1)
    soft(pre_keys(3), 0)
    new("block_landed", 0)
    score(new_keys(0, 0), 0)
    soft(pre_keys(2), 1)
    hide(0, 0)

    def step(i, carry):
        k, k_next = i + i // 2 - i // 3 * 2, i + 1 + (i + 1) // 2 - (i + 1) // 3 * 2

        @pl.when(i < 3)
        def _():
            new("across_landed", k_next)

        score(new_keys(k, 1), 1)
        soft(new_keys(k, 0), 0)
        hide(k, 1)

        @pl.when(i < 3)
        def _():
            new("block_landed", k_next)
            score(new_keys(k_next, 0), 0)
            soft(new_keys(k, 1), 1)
            hide(k_next, 0)

        @pl.when(i == 3)
        def _():
            soft(new_keys(k, 1), 1)
        return carry

    lax.fori_loop(0, 4, step, 0)

    wanted = tab_ref[:, 2 * HALF : 2 * HALF + 1]
    picked = jnp.zeros((toks, WIDTH), jnp.float32)
    for b in range(8):
        row = lax.broadcasted_iota(jnp.int32, (toks, KB), 1).astype(jnp.float32) + float(b * KB)
        pick = jnp.where(row == wanted, 1.0, 0.0).astype(jnp.bfloat16)
        keys = nbuf[b // 4, b % 4].reshape(KB, PADDED)
        picked += jnp.dot(pick, keys[:, :WIDTH], preferred_element_type=jnp.float32)
    pool_ref[...] = picked
    loads[6].wait()
    for h in range(heads):
        cols = pl.ds(h * toks, toks)
        att = (acc[:, cols] / l_s[0:1, cols]).astype(jnp.bfloat16)
        out_ref[:, pl.ds(h * VHEAD, VHEAD)] = lax.dot_general(att, vu_ref[h], (((0,), (0,)), ((), ())), preferred_element_type=jnp.float32).astype(jnp.bfloat16)
    prefix("all_sent")
    new("all_sent")
    for j in (1, 2, 3):
        share(j).wait_send()


def leave(att_ref, rows_ref, out_ref, pool_ref):
    out_ref[...] = att_ref[...]
    pages = pool_ref.shape[0]
    for r in range(0, PAGE, 2):
        pair = [rows_ref[pl.ds((r + e) * pages, pages), :] for e in range(2)]
        pool_ref[:, pl.ds(r * WIDTH, 2 * WIDTH)] = jnp.concatenate(pair, axis=1).astype(jnp.bfloat16)


def per_device(tokens, latent_down, latent_gain, query_nope, query_rope, key_up, value_up, prefix_latent, prefix_length, page_table):
    toks, heads = tokens.shape[0], key_up.shape[0]
    seq = lax.axis_index("seq")
    positions = prefix_length[0] + seq * toks + jnp.arange(toks, dtype=jnp.int32)
    frequency = 10000.0 ** (-jnp.arange(HALF, dtype=jnp.float32) / HALF)
    angle = positions.astype(jnp.float32)[:, None] * frequency[None, :]
    pages = toks // PAGE
    slots = seq * pages + jnp.arange(toks, dtype=jnp.int32) % pages
    count = page_table.shape[0]
    page = jnp.sum(jnp.where(page_table[None, :] == slots[:, None], jnp.arange(count, dtype=jnp.int32)[None, :], 0), axis=1)
    row = (page * PAGE + jnp.arange(toks, dtype=jnp.int32) // pages).astype(jnp.float32)
    table = jnp.concatenate([jnp.cos(angle), jnp.sin(angle), jnp.broadcast_to(row[:, None], (toks, 2 * HALF))], axis=1)
    rows, prow = toks // 4, prefix_latent.shape[0] // 4
    grid = (2, 4, 4, 2, 2)
    queries = heads * toks
    vm, sm, hbm = (pl.BlockSpec(memory_space=m) for m in (pltpu.VMEM, pltpu.SMEM, pl.ANY))
    bf, f32, dma = jnp.bfloat16, jnp.float32, pltpu.SemaphoreType.DMA
    down = latent_down.T
    attended, pool = pl.pallas_call(
        functools.partial(kernel, heads, toks),
        out_shape=[jax.ShapeDtypeStruct((toks, heads * VHEAD), bf), jax.ShapeDtypeStruct((toks, WIDTH), f32)],
        in_specs=[sm, vm, vm] + [hbm] * 7, out_specs=[vm, vm],
        scratch_shapes=[
            pltpu.VMEM((*grid, prow, PADDED), bf), pltpu.VMEM((*grid, rows, PADDED), bf),
            pltpu.VMEM((prow, WIDTH), bf), pltpu.VMEM((toks, PADDED), bf), pltpu.VMEM((3, rows, PADDED), bf),
            pltpu.VMEM(tokens.shape, bf), pltpu.VMEM(down.shape, bf),
            pltpu.VMEM(query_nope.shape, bf), pltpu.VMEM(query_rope.shape, bf), pltpu.VMEM(key_up.shape, bf), pltpu.VMEM(value_up.shape, bf),
            pltpu.VMEM((PADDED, queries), bf), pltpu.VMEM((LATENT, queries), f32), pltpu.VMEM((8, queries), f32), pltpu.VMEM((8, queries), f32),
            pltpu.VMEM((2, KB, queries), f32), pltpu.VMEM((LATENT, KB), bf),
            dma((7,)), dma((23,)), dma((23,)), dma((23,)), dma((23,)), dma((3,)), dma((3,))],
        compiler_params=pltpu.CompilerParams(vmem_limit_bytes=63 << 20, collective_id=0, has_side_effects=True), name="latent_attention",
    )(prefix_length, table, latent_gain.reshape(1, LATENT), tokens, down, prefix_latent, query_nope, query_rope, key_up, value_up)
    return tuple(pl.pallas_call(
        leave, out_shape=[jax.ShapeDtypeStruct(attended.shape, bf), jax.ShapeDtypeStruct((pages, PAGE * WIDTH), bf)],
        in_specs=[vm, vm], out_specs=[vm, vm], name="leave",
    )(attended, pool))


def solution(mesh):
    placed = (P("seq", "head"), P("head", None), P(), P("seq", "head"), P("seq", "head"), P("head", None, None), P("head", None, None), P("seq", None), P(), P())
    return jax.shard_map(per_device, mesh=mesh, in_specs=placed, out_specs=(P("seq", "head"), P("seq", None)), check_vma=False)
```

```python
import functools
import jax
import jax.numpy as jnp
from jax import lax
from jax.experimental import pallas as pl
from jax.experimental.pallas import tpu as pltpu
from jax.sharding import PartitionSpec as P
LATENT, ROPE, NOPE, VHEAD, PAGE = 512, 64, 128, 128, 16
WIDTH = LATENT + ROPE
HALF = ROPE // 2
PADDED = 640
KB = 512
SCALE = (NOPE + ROPE) ** -0.5 * 1.4426950408889634
NEG = -1e30
ALL = slice(None)


def place(chip, core):
    y_hi, y_lo = chip["y"] // 2, chip["y"] % 2
    return {"seq": y_lo * 16 + chip["z"] * 4 + chip["x"], "head": y_hi * 2 + core}


def view(buf, chip, core, lanes):
    y = chip["y"]
    y_lo, y_hi = (ALL, ALL) if isinstance(y, slice) else (y % 2, y // 2)
    return buf.at[y_lo, chip["z"], chip["x"], y_hi, core, :, lanes]


class Spread:
    cross = 5

    def __init__(self, buf, lanes, order, here, core, send, recv):
        self.buf, self.lanes, self.order = buf, lanes, order
        self.here, self.core, self.send, self.recv = here, core, send, recv

    def copy(self, chip, slot, to, core):
        ref = view(self.buf, chip, self.core, self.lanes)
        return pltpu.make_async_remote_copy(
            src_ref=ref, dst_ref=ref, send_sem=self.send.at[slot], recv_sem=self.recv.at[slot],
            device_id=place(to, core), device_id_type=pl.DeviceIdType.MESH)

    def landed(self, chip, slot):
        ref = view(self.buf, chip, self.core, self.lanes)
        pltpu.make_async_remote_copy(
            src_ref=ref, dst_ref=ref, send_sem=self.send.at[slot], recv_sem=self.recv.at[slot],
            device_id=place(self.here, 1 - self.core), device_id_type=pl.DeviceIdType.MESH).wait_recv()

    def shifted(self, dim, j):
        return {**self.here, dim: (self.here[dim] + j + 4) % 4}

    def group(self, depth, chip):
        return {**chip, **{d: ALL for d in self.order[:depth]}}

    def ring(self, depth):
        dim = self.order[depth]
        for j in (1, 3, 2):
            self.copy(self.group(depth, self.here), 3 * depth + j - 1, self.shifted(dim, j), self.core).start()

    def ring_landed(self, depth):
        dim = self.order[depth]
        for j in (1, 3, 2):
            self.landed(self.group(depth, self.shifted(dim, -j)), 3 * depth + j - 1)

    def other(self, chip, slot):
        self.copy(self.group(2, chip), slot, self.here, 1 - self.core).start()

    def across(self):
        for j in (1, 3, 2):
            self.copy(self.group(2, self.here), self.cross + j, self.shifted(self.order[2], j), self.core).start()
        self.other(self.here, self.cross + 4)

    def across_landed(self, k):
        chip = self.shifted(self.order[2], k)
        self.landed(self.group(2, chip), self.cross + (4 - k) % 4)
        self.other(chip, self.cross + 4 + k)

    def twin(self):
        return Spread(self.buf, self.lanes, self.order, self.here, 1 - self.core, self.send, self.recv)

    def block_landed(self, k):
        twin = self.twin()
        twin.landed(twin.group(2, twin.shifted(twin.order[2], k)), self.cross + 4 + k)

    def near_sent(self):
        for depth in (0, 1):
            for j in (1, 2, 3):
                self.copy(self.group(depth, self.here), 3 * depth + j - 1, self.shifted(self.order[depth], j), self.core).wait_send()

    def all_sent(self):
        self.near_sent()
        for j in (1, 2, 3):
            self.copy(self.group(2, self.here), self.cross + j, self.shifted(self.order[2], j), self.core).wait_send()
        for k in range(4):
            self.copy(self.group(2, self.shifted(self.order[2], k)), self.cross + 4 + k, self.here, 1 - self.core).wait_send()


PLANES = (("z", "x", "y"), ("x", "y", "z"))


class Plane(Spread):
    cross = 15

    def __init__(self, buf, here, core, send, recv):
        super().__init__(buf, ALL, PLANES[core], here, core, send, recv)

    def twin(self):
        return Plane(self.buf, self.here, 1 - self.core, self.send, self.recv)

    def near(self, i, j):
        a, b, _ = self.order
        return {**self.here, a: (self.here[a] + i + 4) % 4, b: (self.here[b] + j + 4) % 4}

    def spots(self):
        return [(i, j) for i in (1, 3, 0, 2) for j in (1, 3, 0, 2) if i or j]

    def plane(self):
        for i, j in self.spots():
            self.copy(self.here, 4 * i + j, self.near(i, j), self.core).start()

    def plane_landed(self):
        for i, j in self.spots():
            self.landed(self.near(-i, -j), 4 * i + j)

    def near_sent(self):
        for i, j in self.spots():
            self.copy(self.here, 4 * i + j, self.near(i, j), self.core).wait_send()


def position():
    seq, head = lax.axis_index("seq"), lax.axis_index("head")
    here = {"x": seq % 4, "y": (head // 2) * 2 + seq // 16, "z": (seq // 4) % 4}
    return here, head % 2, head


def greet(here, core):
    barrier = pltpu.get_barrier_semaphore()

    def signal(chip, c):
        pl.semaphore_signal(barrier, inc=1, device_id=place(chip, c), device_id_type=pl.DeviceIdType.MESH)

    for d in "xyz":
        for j in (1, 2, 3):
            signal({**here, d: (here[d] + j) % 4}, core)
    signal(here, 1 - core)
    signal({**here, "y": (here["y"] + 2) % 4}, 1 - core)
    for c in range(2):
        @pl.when(core == c)
        def _():
            a, b, _ = PLANES[c]
            for i in (1, 2, 3):
                for j in (1, 2, 3):
                    signal({**here, a: (here[a] + i) % 4, b: (here[b] + j) % 4}, c)


def greeted():
    pl.semaphore_wait(pltpu.get_barrier_semaphore(), 20)


def finish(mixed, gain, cos, sin, seq):
    latent, a, b = mixed[:, :LATENT], mixed[:, LATENT : LATENT + HALF], mixed[:, LATENT + HALF : WIDTH]
    normed = latent * lax.rsqrt(jnp.mean(latent * latent, axis=1, keepdims=True) + 1e-06) * gain
    column = lax.broadcasted_iota(jnp.int32, (mixed.shape[0], PADDED - WIDTH), 1)
    spare = jnp.where(column == 1 + seq, 1.0, 0.0)
    return jnp.concatenate([normed, a * cos - b * sin, a * sin + b * cos, spare], axis=1).astype(jnp.bfloat16)


def kernel(heads, toks, len_ref, tab_ref, gain_ref, tok_hbm, down_hbm, pre_hbm, qn_hbm, qr_hbm, ku_hbm, vu_hbm,
           out_ref, pool_ref, pbuf, nbuf, pown, part, parts, tok_ref, down_ref, qn_ref, qr_ref, ku_ref, vu_ref,
           qt, acc, m_s, l_s, sb, vt, in_sem, pre_send, pre_recv, send, recv, rs_send, rs_recv):
    here, core, head = position()
    seq = lax.axis_index("seq")
    rows, prow = nbuf.shape[5], pbuf.shape[5]
    mine = (here["y"] % 2, here["z"], here["x"], here["y"] // 2, core)
    loads = [pltpu.make_async_copy(src, dst, in_sem.at[i]) for i, (src, dst) in enumerate((
        (tok_hbm, tok_ref), (down_hbm, down_ref), (pre_hbm.at[pl.ds(head * prow, prow), :], pown),
        (qn_hbm, qn_ref), (ku_hbm, ku_ref), (qr_hbm, qr_ref), (vu_hbm, vu_ref)))]
    for load in loads:
        load.start()
    greet(here, core)
    def planes(buf, sends, recvs):
        def run(name, *args):
            for c in range(2):
                @pl.when(core == c)
                def _():
                    getattr(Plane(buf, here, c, sends, recvs), name)(*args)
        return run

    prefix, new = planes(pbuf, pre_send, pre_recv), planes(nbuf, send, recv)

    loads[0].wait()
    loads[1].wait()
    term = lax.dot_general(tok_ref[...], down_ref[...], (((1,), (1,)), ((), ())), preferred_element_type=jnp.float32)
    part[:, :WIDTH] = term.astype(jnp.bfloat16)
    part[:, WIDTH:] = jnp.zeros((part.shape[0], PADDED - WIDTH), jnp.bfloat16)

    def share(j):
        to = (head + j) % 4
        return pltpu.make_async_remote_copy(
            src_ref=part.at[pl.ds(to * rows, rows), :], dst_ref=parts.at[j - 1], send_sem=rs_send.at[j - 1], recv_sem=rs_recv.at[j - 1],
            device_id={"seq": seq, "head": to}, device_id_type=pl.DeviceIdType.MESH)

    def lift(h):
        cols = pl.ds(h * toks, toks)
        lifted = jnp.dot(qn_ref[:, pl.ds(h * NOPE, NOPE)], ku_ref[h], preferred_element_type=jnp.float32)
        qt[:LATENT, cols] = lifted.T.astype(jnp.bfloat16)

    turn = tab_ref[...].T

    def rotate(g):
        cos, sin = turn[:HALF], turn[HALF : 2 * HALF]
        both = qr_ref[:, pl.ds(g * 2 * ROPE, 2 * ROPE)].astype(jnp.float32).T
        for e in range(2):
            a, b = both[ROPE * e : ROPE * e + HALF], both[ROPE * e + HALF : ROPE * (e + 1)]
            cols = pl.ds((2 * g + e) * toks, toks)
            qt[LATENT : LATENT + HALF, cols] = (a * cos - b * sin).astype(jnp.bfloat16)
            qt[LATENT + HALF : WIDTH, cols] = (a * sin + b * cos).astype(jnp.bfloat16)

    loads[2].wait()
    spare = (prow, PADDED - WIDTH)
    row = seq * 4 * prow + head * prow + lax.broadcasted_iota(jnp.int32, spare, 0)
    dead = (row >= len_ref[0]) & (lax.broadcasted_iota(jnp.int32, spare, 1) == 0)
    pbuf[mine] = jnp.concatenate([pown[...], jnp.where(dead, NEG, 0.0).astype(jnp.bfloat16)], axis=1)
    loads[3].wait()
    loads[4].wait()
    for h in range(heads // 2):
        lift(h)
    greeted()
    for j in (1, 2, 3):
        share(j).start()
    prefix("plane")
    for h in range(heads // 2, heads):
        lift(h)
    for j in (1, 2, 3):
        share(j).wait_recv()
    own_rows = pl.ds(pl.multiple_of(head * rows, rows), rows)
    mixed = part[own_rows, :].astype(jnp.float32)
    for j in range(3):
        mixed += parts[j].astype(jnp.float32)
    nbuf[mine] = finish(mixed, gain_ref[...], tab_ref[own_rows, :HALF], tab_ref[own_rows, HALF : 2 * HALF], seq)
    new("plane")
    prefix("plane_landed")
    prefix("across")
    loads[5].wait()
    for g in range(heads // 2):
        rotate(g)
    spare_row = lax.broadcasted_iota(jnp.int32, (PADDED - WIDTH, heads * toks), 0)
    late = (spare_row > 1 + seq) & (spare_row < 33)
    qt[WIDTH:, :] = jnp.where(spare_row == 0, 1.0, jnp.where(late, NEG, 0.0)).astype(jnp.bfloat16)
    m_s[...] = jnp.full_like(m_s, NEG)
    l_s[...] = jnp.zeros_like(l_s)
    acc[...] = jnp.zeros_like(acc)


    def pre_keys(k):
        y, z = (here["y"] + k) % 4, (here["z"] + k) % 4
        even = pbuf[y % 2, :, :, y // 2, 0].reshape(KB // 2, PADDED)
        odd = pbuf[:, z, :, :, 1].reshape(KB // 2, PADDED)
        return jnp.concatenate([even, odd], axis=0)

    def new_keys(k, odd):
        y, z = (here["y"] + k) % 4, (here["z"] + k) % 4
        if odd:
            return nbuf[:, z, :, :, 1].reshape(KB, PADDED)
        return nbuf[y % 2, :, :, y // 2, 0].reshape(KB, PADDED)

    def score(keys, slot):
        sb[slot] = jnp.dot(keys, qt[...], preferred_element_type=jnp.float32)

    def hide(k, odd):
        count = 2 * rows if odd else rows
        start = ((here["y"] % 2 if odd else here["z"]) * 4 + here["x"]) * count
        own = pl.ds(pl.multiple_of(start, rows), count)
        m = lax.broadcasted_iota(jnp.int32, (count, toks), 0)
        y_hi = m // rows if odd else (here["y"] + k) % 4 // 2
        live = (y_hi * 2 + odd) * rows + m % rows <= lax.broadcasted_iota(jnp.int32, (count, toks), 1)
        for h in range(heads):
            cols = pl.ds(h * toks, toks)
            sb[odd, own, cols] = jnp.where(live, sb[odd, own, cols], NEG)

    def score_pre(k, slot):
        prefix("block_landed", k)
        score(pre_keys(k), slot)

    def soft(keys, slot):
        vt[...] = keys[:, :LATENT].T
        s = sb[slot]
        old = m_s[0:1]
        top = jnp.maximum(old, jnp.max(s, axis=0, keepdims=True))
        fade = jnp.exp2((old - top) * SCALE)
        m_s[0:1] = top
        w = jnp.exp2((s - top) * SCALE)
        l_s[0:1] = l_s[0:1] * fade + jnp.sum(w, axis=0, keepdims=True)
        acc[...] = acc[...] * fade + jnp.dot(vt[...], w.astype(jnp.bfloat16), preferred_element_type=jnp.float32)

    score_pre(0, 0)
    new("plane_landed")
    new("across")
    soft(pre_keys(0), 0)
    prefix("across_landed", 1)
    prefix("across_landed", 3)
    score_pre(1, 1)
    prefix("across_landed", 2)
    prefix("block_landed", 3)
    score(pre_keys(3), 0)
    soft(pre_keys(1), 1)
    prefix("block_landed", 2)
    score(pre_keys(2), 1)
    soft(pre_keys(3), 0)
    new("block_landed", 0)
    score(new_keys(0, 0), 0)
    soft(pre_keys(2), 1)
    hide(0, 0)

    def step(i, carry):
        k, k_next = i + i // 2 - i // 3 * 2, i + 1 + (i + 1) // 2 - (i + 1) // 3 * 2

        @pl.when(i < 3)
        def _():
            new("across_landed", k_next)

        score(new_keys(k, 1), 1)
        soft(new_keys(k, 0), 0)
        @pl.when(i == 0)
        def _():
            hide(0, 1)

        @pl.when(i < 3)
        def _():
            new("block_landed", k_next)
            score(new_keys(k_next, 0), 0)
            soft(new_keys(k, 1), 1)
            @pl.when(i == 2)
            def _():
                hide(2, 0)

        @pl.when(i == 3)
        def _():
            soft(new_keys(k, 1), 1)
        return carry

    lax.fori_loop(0, 4, step, 0)

    wanted = tab_ref[:, 2 * HALF : 2 * HALF + 1]
    picked = jnp.zeros((toks, WIDTH), jnp.float32)
    for b in range(8):
        row = lax.broadcasted_iota(jnp.int32, (toks, KB), 1).astype(jnp.float32) + float(b * KB)
        pick = jnp.where(row == wanted, 1.0, 0.0).astype(jnp.bfloat16)
        keys = nbuf[b // 4, b % 4].reshape(KB, PADDED)
        picked += jnp.dot(pick, keys[:, :WIDTH], preferred_element_type=jnp.float32)
    pool_ref[...] = picked
    loads[6].wait()
    for h in range(heads):
        cols = pl.ds(h * toks, toks)
        att = (acc[:, cols] / l_s[0:1, cols]).astype(jnp.bfloat16)
        out_ref[:, pl.ds(h * VHEAD, VHEAD)] = lax.dot_general(att, vu_ref[h], (((0,), (0,)), ((), ())), preferred_element_type=jnp.float32).astype(jnp.bfloat16)
    prefix("all_sent")
    new("all_sent")
    for j in (1, 2, 3):
        share(j).wait_send()


def leave(att_ref, rows_ref, out_ref, pool_ref):
    out_ref[...] = att_ref[...]
    pages = pool_ref.shape[0]
    for r in range(0, PAGE, 2):
        pair = [rows_ref[pl.ds((r + e) * pages, pages), :] for e in range(2)]
        pool_ref[:, pl.ds(r * WIDTH, 2 * WIDTH)] = jnp.concatenate(pair, axis=1).astype(jnp.bfloat16)


def per_device(tokens, latent_down, latent_gain, query_nope, query_rope, key_up, value_up, prefix_latent, prefix_length, page_table):
    toks, heads = tokens.shape[0], key_up.shape[0]
    seq = lax.axis_index("seq")
    positions = prefix_length[0] + seq * toks + jnp.arange(toks, dtype=jnp.int32)
    frequency = 10000.0 ** (-jnp.arange(HALF, dtype=jnp.float32) / HALF)
    angle = positions.astype(jnp.float32)[:, None] * frequency[None, :]
    pages = toks // PAGE
    slots = seq * pages + jnp.arange(toks, dtype=jnp.int32) % pages
    count = page_table.shape[0]
    page = jnp.sum(jnp.where(page_table[None, :] == slots[:, None], jnp.arange(count, dtype=jnp.int32)[None, :], 0), axis=1)
    row = (page * PAGE + jnp.arange(toks, dtype=jnp.int32) // pages).astype(jnp.float32)
    table = jnp.concatenate([jnp.cos(angle), jnp.sin(angle), jnp.broadcast_to(row[:, None], (toks, 2 * HALF))], axis=1)
    rows, prow = toks // 4, prefix_latent.shape[0] // 4
    grid = (2, 4, 4, 2, 2)
    queries = heads * toks
    vm, sm, hbm = (pl.BlockSpec(memory_space=m) for m in (pltpu.VMEM, pltpu.SMEM, pl.ANY))
    bf, f32, dma = jnp.bfloat16, jnp.float32, pltpu.SemaphoreType.DMA
    down = latent_down.T
    attended, pool = pl.pallas_call(
        functools.partial(kernel, heads, toks),
        out_shape=[jax.ShapeDtypeStruct((toks, heads * VHEAD), bf), jax.ShapeDtypeStruct((toks, WIDTH), f32)],
        in_specs=[sm, vm, vm] + [hbm] * 7, out_specs=[vm, vm],
        scratch_shapes=[
            pltpu.VMEM((*grid, prow, PADDED), bf), pltpu.VMEM((*grid, rows, PADDED), bf),
            pltpu.VMEM((prow, WIDTH), bf), pltpu.VMEM((toks, PADDED), bf), pltpu.VMEM((3, rows, PADDED), bf),
            pltpu.VMEM(tokens.shape, bf), pltpu.VMEM(down.shape, bf),
            pltpu.VMEM(query_nope.shape, bf), pltpu.VMEM(query_rope.shape, bf), pltpu.VMEM(key_up.shape, bf), pltpu.VMEM(value_up.shape, bf),
            pltpu.VMEM((PADDED, queries), bf), pltpu.VMEM((LATENT, queries), f32), pltpu.VMEM((8, queries), f32), pltpu.VMEM((8, queries), f32),
            pltpu.VMEM((2, KB, queries), f32), pltpu.VMEM((LATENT, KB), bf),
            dma((7,)), dma((23,)), dma((23,)), dma((23,)), dma((23,)), dma((3,)), dma((3,))],
        compiler_params=pltpu.CompilerParams(vmem_limit_bytes=63 << 20, collective_id=0, has_side_effects=True), name="latent_attention",
    )(prefix_length, table, latent_gain.reshape(1, LATENT), tokens, down, prefix_latent, query_nope, query_rope, key_up, value_up)
    return tuple(pl.pallas_call(
        leave, out_shape=[jax.ShapeDtypeStruct(attended.shape, bf), jax.ShapeDtypeStruct((pages, PAGE * WIDTH), bf)],
        in_specs=[vm, vm], out_specs=[vm, vm], name="leave",
    )(attended, pool))


def solution(mesh):
    placed = (P("seq", "head"), P("head", None), P(), P("seq", "head"), P("seq", "head"), P("head", None, None), P("head", None, None), P("seq", None), P(), P())
    return jax.shard_map(per_device, mesh=mesh, in_specs=placed, out_specs=(P("seq", "head"), P("seq", None)), check_vma=False)
```
